32 devices in a mesh: section: 4 (over z), seq: 4 (over y, x), tp: 2 (over core).
Axes of the slice: x: 2, y: 2, z: 4, core: 2. Of those that a mesh axis runs over, the one named last changes fastest.
Arguments:
- queries: bfloat16 [4, 512, 8192], P('section', 'seq', 'tp'), may hold values from -48 to 48
- keys: bfloat16 [4, 512, 1024], P('section', 'seq'), may hold values from -8 to 8
- values: bfloat16 [4, 512, 1024], P('section', 'seq'), may hold values from -6 to 6
- out_grad: bfloat16 [4, 512, 8192], P('section', 'seq', 'tp'), may hold values from -6 to 6
- rand_blocks: int32 [8, 3], replicated, may hold values from 0 to 7, as said below
- global_blocks: int32 [2], replicated, may hold values from 0 to 7, as said below
- win_reach: int32 [64], replicated, may hold values from 0 to 1, as said below
Outputs:
- query_upstream: bfloat16 [4, 512, 8192], P('section', 'seq', 'tp')
- keyval_upstream: bfloat16 [4, 512, 2048], P('section', 'seq', 'tp')
The draws below stay inside these ranges and needn't reach their ends.
Inputs may be any that keep to these rules, and one draw needn't show every extreme that they name: `rand_blocks`: block b belongs to index b // 2 of seq. Over the 2 query blocks of one index of seq, the blocks listed here together with their window neighbours +-1 .. +-1 include at most 3 that belong to any one other index, and exactly 3 from some other index, in every such group of rows. `global_blocks`: 2 distinct blocks; the last block of the sequence is one of them. `win_reach`: some head reaches 1 block and some head 0.
All inputs are finite; a program needn't handle non-finite values.
Results may differ from the reference program's by a relative error of at most 0.015.
Values may be sent and summed in bfloat16 or wider, within the bound.
A program may use at most 128 MiB of HBM per device.

```python
import jax
import jax.numpy as jnp
from jax import lax

QUERY_HEADS = 64
KV_HEADS = 8
HEAD_DIM = 128
BLOCK_LEN = 64
WINDOW = 1
GLOBALS = 2
RANDOM = 3
BLOCKS_DEV = 2
SECTIONS = 4
ALL_BLOCKS = 8
TOKENS = 512
KEY_SLOTS = 8
CAPACITY = 3
N_SEQ = 4
N_TP = 2


def key_field(key):
    field_shape = (SECTIONS, TOKENS, KV_HEADS * HEAD_DIM)
    base_field = jax.random.truncated_normal(jax.random.fold_in(key, 101), -6.0, 6.0, field_shape, jnp.float32)
    return base_field


def draw_keys(key, part):
    return key_field(key).astype(jnp.bfloat16)


def draw_queries(key, part):
    field_shape = (SECTIONS, TOKENS, QUERY_HEADS * HEAD_DIM)
    base_field = jax.random.truncated_normal(jax.random.fold_in(key, 202), -6.0, 6.0, field_shape, jnp.float32)
    return base_field.astype(jnp.bfloat16)


def draw_rand_blocks(key, part):
    copies = N_SEQ * CAPACITY
    pick_count = BLOCKS_DEV * RANDOM
    owner_list = jnp.repeat(jnp.arange(N_SEQ, dtype=jnp.int32), CAPACITY)
    copy_list = jnp.tile(jnp.arange(CAPACITY, dtype=jnp.int32), N_SEQ)
    position = jnp.arange(copies, dtype=jnp.int32)

    def one_shard(shard_index):
        shard_key = jax.random.fold_in(key, shard_index + 17)
        left_shard = (shard_index + N_SEQ - 1) % N_SEQ
        right_shard = (shard_index + 1) % N_SEQ
        dropped = ((owner_list == left_shard) | (owner_list == right_shard)) & (copy_list >= CAPACITY - WINDOW)
        forced_owner = (shard_index + 2 + jax.random.randint(jax.random.fold_in(shard_key, 1), (), 0, N_SEQ - 3)) % N_SEQ
        noise_bits = jax.random.randint(jax.random.fold_in(shard_key, 2), (copies,), 1, 1 << 20)
        sort_score = jnp.where(owner_list == forced_owner, 0, noise_bits)
        sort_score = jnp.where(dropped, 1 << 21, sort_score) * copies + position
        sort_order = jnp.argsort(sort_score)
        picked = owner_list[sort_order[:pick_count]]
        shuffled = picked[jax.random.permutation(jax.random.fold_in(shard_key, 3), pick_count)]
        offset = jax.random.randint(jax.random.fold_in(shard_key, 4), (pick_count,), 0, BLOCKS_DEV)
        return (shuffled * BLOCKS_DEV + offset).reshape(BLOCKS_DEV, RANDOM)
    block_table = jax.vmap(one_shard)(jnp.arange(N_SEQ, dtype=jnp.int32))
    return block_table.reshape(ALL_BLOCKS, RANDOM).astype(jnp.int32)


def draw_global_blocks(key, part):
    others = jax.random.permutation(jax.random.fold_in(key, 5), ALL_BLOCKS - 1)[:GLOBALS - 1].astype(jnp.int32)
    listed = jnp.concatenate([jnp.full((1,), ALL_BLOCKS - 1, jnp.int32), others])
    order = jax.random.permutation(jax.random.fold_in(key, 8), GLOBALS)
    return listed[order].astype(jnp.int32)


def draw_win_reach(key, part):
    base_reach = jax.random.randint(jax.random.fold_in(key, 6), (QUERY_HEADS,), 0, WINDOW + 1)
    sort_order = jax.random.permutation(jax.random.fold_in(key, 7), QUERY_HEADS)
    return base_reach.at[sort_order[0]].set(WINDOW).at[sort_order[1]].set(0).astype(jnp.int32)


def steps_of(own_key, shape, shards, low, top_value):
    loudness = 1.0
    for dim, blocks in shards:
        heights = jax.random.uniform(jax.random.fold_in(jax.random.fold_in(own_key, 6), dim), (blocks,), jnp.float32, low / len(shards), top_value / len(shards))
        loudness = loudness * jnp.repeat(jnp.exp(heights), shape[dim] // blocks).reshape((-1,) + (1,) * (len(shape) - 1 - dim))
    return loudness


def centred(key, dims, scale, reach, cuts=(), held_as=jnp.bfloat16):
    factor_of = steps_of(key, dims, cuts, -0.22, 0.18) if cuts else 1.0
    values = jax.random.normal(key, dims, jnp.float32) * scale * factor_of
    return jnp.minimum(jnp.maximum(values, -reach), reach).astype(held_as)


def setup_inputs(seed: int = 0) -> dict:
    streams_of = jax.random.split(jax.random.key(seed), 8)
    queries = draw_queries(jax.random.fold_in(streams_of[7], 71), 0)
    keys = draw_keys(jax.random.fold_in(streams_of[7], 71), 0)
    values = centred(streams_of[2], (SECTIONS, TOKENS, KV_HEADS * HEAD_DIM), 1.0, 6.0, ((0, 4), (1, 4)))
    out_grad = centred(streams_of[3], (SECTIONS, TOKENS, QUERY_HEADS * HEAD_DIM), 1.0, 6.0, ((0, 4), (1, 4), (2, 2)))
    rand_blocks = draw_rand_blocks(jax.random.fold_in(streams_of[7], 71), 0)
    global_blocks = draw_global_blocks(jax.random.fold_in(streams_of[7], 71), 0)
    win_reach = draw_win_reach(jax.random.fold_in(streams_of[7], 71), 0)
    return {"queries": queries, "keys": keys, "values": values, "out_grad": out_grad, "rand_blocks": rand_blocks, "global_blocks": global_blocks, "win_reach": win_reach}


def slot_table(rand_blocks, global_blocks):
    block_ids = jnp.arange(ALL_BLOCKS, dtype=jnp.int32)
    columns = []
    inside = []
    reach_need = []
    for o in range(-WINDOW, WINDOW + 1):
        shifted = block_ids + o
        columns.append(jnp.clip(shifted, 0, ALL_BLOCKS - 1).astype(jnp.int32))
        inside.append((shifted >= 0) & (shifted < ALL_BLOCKS))
        reach_need.append(abs(o))
    for g in range(GLOBALS):
        columns.append(jnp.zeros((ALL_BLOCKS,), jnp.int32) + global_blocks[g].astype(jnp.int32))
        inside.append(jnp.ones((ALL_BLOCKS,), bool))
        reach_need.append(0)
    for r in range(RANDOM):
        columns.append(rand_blocks[:, r].astype(jnp.int32))
        inside.append(jnp.ones((ALL_BLOCKS,), bool))
        reach_need.append(0)
    return jnp.stack(columns, axis=1), jnp.stack(inside, axis=1), jnp.array(reach_need, jnp.int32)


def block_grads(query_block, grad_block, key_value, allowed):
    kv_width = KV_HEADS * HEAD_DIM
    repeats = QUERY_HEADS // KV_HEADS
    group_heads = repeats // N_TP
    query_heads = query_block.astype(jnp.float32).reshape(BLOCK_LEN, repeats, KV_HEADS, HEAD_DIM)
    grad_heads = grad_block.astype(jnp.float32).reshape(BLOCK_LEN, repeats, KV_HEADS, HEAD_DIM)
    key_heads = key_value[..., :kv_width].astype(jnp.float32).reshape(KEY_SLOTS * BLOCK_LEN, KV_HEADS, HEAD_DIM)
    value_heads = key_value[..., kv_width:].astype(jnp.float32).reshape(KEY_SLOTS * BLOCK_LEN, KV_HEADS, HEAD_DIM)
    score_scale = HEAD_DIM ** -0.5
    scores = jnp.einsum("qrgd,kgd->grqk", query_heads, key_heads) * score_scale
    row_max = jnp.max(jnp.where(allowed, scores, -jnp.inf), axis=-1, keepdims=True)
    exp_terms = jnp.where(allowed, jnp.exp(scores - row_max), 0.0)
    attn_weights = exp_terms / jnp.sum(exp_terms, axis=-1, keepdims=True)
    weight_grads = jnp.einsum("qrgd,kgd->grqk", grad_heads, value_heads)
    row_delta = jnp.sum(attn_weights * weight_grads, axis=-1, keepdims=True)
    score_grads = attn_weights * (weight_grads - row_delta)
    weights_low = lax.optimization_barrier(attn_weights.astype(jnp.bfloat16)).astype(jnp.float32)
    grads_low = lax.optimization_barrier(score_grads.astype(jnp.bfloat16)).astype(jnp.float32)
    query_grads = jnp.einsum("grqk,kgd->qrgd", grads_low, key_heads) * score_scale
    split_grads = grads_low.reshape(KV_HEADS, N_TP, group_heads, BLOCK_LEN, KEY_SLOTS * BLOCK_LEN)
    split_weights = weights_low.reshape(KV_HEADS, N_TP, group_heads, BLOCK_LEN, KEY_SLOTS * BLOCK_LEN)
    query_split = query_heads.reshape(BLOCK_LEN, N_TP, group_heads, KV_HEADS, HEAD_DIM)
    grad_split = grad_heads.reshape(BLOCK_LEN, N_TP, group_heads, KV_HEADS, HEAD_DIM)
    key_grads = jnp.einsum("gtrqk,qtrgd->tkgd", split_grads, query_split) * score_scale
    value_grads = jnp.einsum("gtrqk,qtrgd->tkgd", split_weights, grad_split)
    slot_parts = jnp.concatenate([key_grads.reshape(N_TP, KEY_SLOTS, BLOCK_LEN, kv_width),
                                  value_grads.reshape(N_TP, KEY_SLOTS, BLOCK_LEN, kv_width)], axis=-1)
    slot_parts = lax.optimization_barrier(slot_parts.astype(jnp.bfloat16)).astype(jnp.float32)
    return query_grads.reshape(BLOCK_LEN, -1).astype(jnp.bfloat16), jnp.sum(slot_parts, axis=0)


def reference(queries, keys, values, out_grad, rand_blocks, global_blocks, win_reach):
    slot_blocks, slot_inside, reach_need = slot_table(rand_blocks, global_blocks)
    repeats = QUERY_HEADS // KV_HEADS
    reach_table = win_reach.astype(jnp.int32).reshape(repeats, KV_HEADS).T
    kv_width = KV_HEADS * HEAD_DIM

    def one_section(arrays):
        query_all, key_all, value_all, grad_all = arrays
        key_value = jnp.concatenate([key_all, value_all], axis=1).reshape(ALL_BLOCKS, BLOCK_LEN, 2 * kv_width)
        query_blocks = query_all.reshape(ALL_BLOCKS, BLOCK_LEN, -1)
        grad_blocks = grad_all.reshape(ALL_BLOCKS, BLOCK_LEN, -1)

        def step(totals, index):
            chosen = slot_blocks[index]
            live = slot_inside[index][None, None, :] & (reach_need[None, None, :] <= reach_table[:, :, None])
            allowed = jnp.broadcast_to(live[:, :, None, :, None], (KV_HEADS, repeats, 1, KEY_SLOTS, BLOCK_LEN))
            allowed = allowed.reshape(KV_HEADS, repeats, 1, KEY_SLOTS * BLOCK_LEN)
            query_grads, parts = block_grads(query_blocks[index], grad_blocks[index], key_value[chosen], allowed)
            return totals.at[chosen].add(parts), query_grads

        start = jnp.zeros((ALL_BLOCKS, BLOCK_LEN, 2 * kv_width), jnp.float32)
        totals, query_grads = lax.scan(step, start, jnp.arange(ALL_BLOCKS, dtype=jnp.int32))
        return query_grads.reshape(TOKENS, -1), totals.reshape(TOKENS, 2 * kv_width).astype(jnp.bfloat16)

    query_all, keyval_all = lax.map(one_section, (queries, keys, values, out_grad))
    query_upstream = jnp.concatenate([query_all[1:], jnp.zeros_like(query_all[:1])], axis=0)
    keyval_upstream = jnp.concatenate([keyval_all[1:], jnp.zeros_like(keyval_all[:1])], axis=0)
    return query_upstream, keyval_upstream
```

```python
import functools
import math

import jax
import jax.numpy as jnp
from jax import lax
from jax.experimental import pallas as pl
from jax.experimental.pallas import tpu as pltpu
from jax.sharding import PartitionSpec as P

HEAD_DIM = 128
BLOCK_LEN = 64
WINDOW = 1
MESH = pl.DeviceIdType.MESH
NT = (((1,), (1,)), ((), ()))
TN = (((0,), (0,)), ((), ()))


def head_cols(h):
    return pl.ds(pl.multiple_of(h * HEAD_DIM, HEAD_DIM), HEAD_DIM)


def kernel(
    sections, shards, groups, repeats, rand_hbm, glob_hbm, reach_hbm,
    q_hbm, do_hbm, k_hbm, v_hbm, outq_ref, outkv_ref,
    q_ref, do_ref, kv_all, stage, sib, part, landed, dq, final,
    g_send, g_recv, f_send, f_recv, x_send, x_recv, r_send, r_recv,
    zq_send, zq_recv, zk_send, zk_recv, own_sem, load_sem,
    rand_ref, glob_ref, reach_ref,
):
    section = lax.axis_index("section")
    me = lax.axis_index("seq")
    t = lax.axis_index("tp")
    peers = shards - 1
    tokens = q_ref.shape[0]
    local_blocks = tokens // BLOCK_LEN
    all_blocks = local_blocks * shards
    scale = HEAD_DIM ** -0.5

    def rows(shard):
        return pl.ds(pl.multiple_of(shard * tokens, tokens), tokens)

    def remote(src, dst, send, recv, device):
        return pltpu.make_async_remote_copy(
            src_ref=src, dst_ref=dst, send_sem=send, recv_sem=recv,
            device_id=device, device_id_type=MESH,
        )

    def own(half, g, source):
        return pltpu.make_async_copy(
            source.at[:, head_cols(g)], kv_all.at[half, g, rows(me)], own_sem.at[half, g]
        )

    def gather(g, d, shard, source=None):
        block = kv_all.at[t, g, rows(shard)]
        source = block if source is None else source.at[:, head_cols(g)]
        to = lax.rem(me + d, shards)
        return remote(source, block, g_send.at[g, d - 1], g_recv.at[g, d - 1], {"seq": to})

    def forward(g, d, half):
        block = kv_all.at[half, g, rows(lax.rem(me - d + shards, shards))]
        return remote(block, block, f_send.at[g, d - 1], f_recv.at[g, d - 1], {"tp": 1 - t})

    def exchange(g):
        return remote(stage.at[1 - t, g], sib.at[g], x_send.at[g], x_recv.at[g], {"tp": 1 - t})

    def scatter(g, d):
        to = lax.rem(me + d, shards)
        return remote(
            part.at[g, rows(to)], landed.at[g, d - 1],
            r_send.at[g, d - 1], r_recv.at[g, d - 1], {"seq": to},
        )

    def hand_query(g, r):
        cols = head_cols(r * groups + g)
        return remote(
            dq.at[:, cols], outq_ref.at[0, :, cols],
            zq_send.at[g, r], zq_recv.at[g, r], {"section": section - 1},
        )

    def hand_keyval(g):
        cols = head_cols(g)
        return remote(
            final.at[:, cols], outkv_ref.at[0, :, cols],
            zk_send.at[g], zk_recv.at[g], {"section": section - 1},
        )

    @pl.loop(0, groups)
    def _(g):
        own(0, g, k_hbm).start()
        own(1, g, v_hbm).start()

    load_query = pltpu.make_async_copy(q_hbm, q_ref, load_sem.at[0])
    load_grad = pltpu.make_async_copy(do_hbm, do_ref, load_sem.at[1])
    tables = [
        pltpu.make_async_copy(source, target, load_sem.at[2 + i])
        for i, (source, target) in enumerate(
            ((rand_hbm, rand_ref), (glob_hbm, glob_ref), (reach_hbm, reach_ref))
        )
    ]
    for table in tables:
        table.start()
    load_query.start()
    load_grad.start()

    barrier = pltpu.get_barrier_semaphore()

    @pl.loop(1, shards)
    def _(d):
        pl.semaphore_signal(
            barrier, inc=1, device_id={"seq": lax.rem(me + d, shards)}, device_id_type=MESH
        )

    pl.semaphore_signal(barrier, inc=1, device_id={"tp": 1 - t}, device_id_type=MESH)

    @pl.when(section < sections - 1)
    def _():
        pl.semaphore_signal(
            barrier, inc=1, device_id={"section": section + 1}, device_id_type=MESH
        )

    below = jnp.where(section > 0, 1, 0)
    pl.semaphore_wait(barrier, peers + 1 + below)

    def spread(g):
        for half, source in ((0, k_hbm), (1, v_hbm)):

            @pl.when(t == half)
            def _():
                @pl.loop(1, shards)
                def _(d):
                    gather(g, d, me, source).start()

    def sent(g):
        @pl.loop(1, shards)
        def _(d):
            gather(g, d, me).wait_send()

    def pass_on(g):
        @pl.loop(1, shards)
        def _(d):
            gather(g, d, lax.rem(me - d + shards, shards)).wait_recv()
            forward(g, d, t).start()

        @pl.when(g + 2 < groups)
        def _():
            spread(g + 2)

    spread(0)
    sent(0)
    spread(1)

    def send_parts(g):
        exchange(g).wait_recv()
        both = stage[t, g].astype(jnp.float32) + sib[g].astype(jnp.float32)
        part[g] = both.astype(jnp.bfloat16)

        @pl.loop(1, shards)
        def _(d):
            scatter(g, d).start()

    for table in tables:
        table.wait()
    chunk = 2
    width = chunk * tokens
    lane = lax.broadcasted_iota(jnp.int32, (all_blocks, width), 1)
    block_id = lax.broadcasted_iota(jnp.int32, (all_blocks, width), 0)
    lane_block = lax.rem(lane, tokens) // BLOCK_LEN
    lane_head = lane // tokens
    query_block = me * local_blocks + lane_block
    distance = jnp.abs(block_id - query_block)
    always = jnp.zeros((all_blocks, width), jnp.float32)
    for i in range(glob_ref.shape[0]):
        always += (block_id == glob_ref[i]).astype(jnp.float32)
    for i in range(rand_ref.shape[0]):
        for j in range(local_blocks):
            named = (lane_block == j) & (block_id == rand_ref[i, me * local_blocks + j])
            always += named.astype(jnp.float32)

    pass_on(0)
    load_query.wait()
    load_grad.wait()

    @pl.loop(0, groups)
    def _(g):
        own(0, g, k_hbm).wait()
        own(1, g, v_hbm).wait()

        @pl.loop(1, shards)
        def _(d):
            forward(g, d, 1 - t).wait_recv()

        keys = kv_all[0, g]
        values = kv_all[1, g]
        key_grads = None
        for c in range(repeats // chunk):
            heads = [c * chunk + i for i in range(chunk)]
            query = jnp.concatenate([q_ref[:, head_cols(r * groups + g)] for r in heads], axis=0)
            grad = jnp.concatenate([do_ref[:, head_cols(r * groups + g)] for r in heads], axis=0)
            reach = jnp.zeros((all_blocks, width), jnp.int32)
            for i, r in enumerate(heads):
                reach = jnp.where(lane_head == i, reach_ref[(t * repeats + r) * groups + g], reach)
            window = (distance <= WINDOW) & (distance <= reach)
            count = always + window.astype(jnp.float32)
            bias = jnp.where(
                count > 0, jnp.log(jnp.maximum(count, 1.0)) * (1.0 / math.log(2.0)), -1e30
            )
            scores = lax.dot_general(keys, query, NT, preferred_element_type=jnp.float32)
            scores = scores.reshape(all_blocks, BLOCK_LEN, width) * (scale / math.log(2.0))
            scores = (scores + bias[:, None, :]).reshape(all_blocks * BLOCK_LEN, width)
            row_max = jnp.max(scores, axis=0, keepdims=True)
            terms = jnp.exp2(scores - row_max)
            weights = terms * (1.0 / jnp.sum(terms, axis=0, keepdims=True))
            weight_grads = lax.dot_general(values, grad, NT, preferred_element_type=jnp.float32)
            delta = jnp.sum(weights * weight_grads, axis=0, keepdims=True)
            grads_low = (weights * (weight_grads - delta)).astype(jnp.bfloat16)
            weights_low = weights.astype(jnp.bfloat16)
            query_grads = lax.dot_general(
                grads_low, keys, TN, preferred_element_type=jnp.float32
            )
            query_grads = (query_grads * scale).astype(jnp.bfloat16)
            for i, r in enumerate(heads):
                dq[:, head_cols(r * groups + g)] = query_grads[i * tokens : (i + 1) * tokens]

            @pl.when(section > 0)
            def _():
                for r in heads:
                    hand_query(g, r).start()

            if c == 0:

                @pl.when(g < groups - 1)
                def _():
                    pass_on(g + 1)


            dk = jnp.dot(grads_low, query, preferred_element_type=jnp.float32)
            dv = jnp.dot(weights_low, grad, preferred_element_type=jnp.float32)
            key_grads = dk if key_grads is None else key_grads + dk
            value_grads = dv if c == 0 else value_grads + dv
        stage[0, g] = (key_grads * scale).astype(jnp.bfloat16)
        stage[1, g] = value_grads.astype(jnp.bfloat16)
        exchange(g).start()

        @pl.when(g > 0)
        def _():
            send_parts(g - 1)

    send_parts(groups - 1)

    @pl.loop(0, groups)
    def _(g):
        @pl.loop(1, shards)
        def _(d):
            scatter(g, d).wait_recv()

        total = part[g, rows(me), :].astype(jnp.float32)
        for d in range(1, shards):
            total += landed[g, d - 1].astype(jnp.float32)
        final[:, head_cols(g)] = total.astype(jnp.bfloat16)

        @pl.when(section > 0)
        def _():
            hand_keyval(g).start()

    @pl.loop(1, groups)
    def _(g):
        sent(g)

    @pl.loop(0, groups)
    def _(g):
        @pl.loop(1, shards)
        def _(d):
            scatter(g, d).wait_send()
            forward(g, d, t).wait_send()

        exchange(g).wait_send()

        @pl.when(section > 0)
        def _():
            for r in range(repeats):
                hand_query(g, r).wait_send()
            hand_keyval(g).wait_send()

        @pl.when(section < sections - 1)
        def _():
            for r in range(repeats):
                hand_query(g, r).wait_recv()
            hand_keyval(g).wait_recv()


def copy_out(sections, pieces, q_in, kv_in, q_out, kv_out, blank, out_sem):
    section = lax.axis_index("section")
    size = q_in.shape[1] // pieces
    width = kv_in.shape[2]

    def stores(held):
        copies = []
        for k, (source, target) in enumerate(((q_in, q_out), (kv_in, kv_out))):
            for i in range(pieces):
                piece = pl.ds(i * size, size)
                src = source.at[0, piece] if held is None else held.at[:, pl.ds(0, source.shape[2])]
                copies.append(
                    pltpu.make_async_copy(src, target.at[0, piece], out_sem.at[k * pieces + i])
                )
        return copies

    @pl.when(section < sections - 1)
    def _():
        for store in stores(None):
            store.start()

    @pl.when(section == sections - 1)
    def _():
        blank[...] = jnp.zeros_like(blank)
        for store in stores(blank):
            store.start()

    for store in stores(None):
        store.wait()


def on_device(queries, keys, values, out_grad, rand_blocks, global_blocks, win_reach):
    sections = lax.axis_size("section")
    shards = lax.axis_size("seq")
    tokens = queries.shape[1]
    kv_width = keys.shape[2]
    groups = kv_width // HEAD_DIM
    repeats = queries.shape[2] // kv_width
    length = tokens * shards
    peers = shards - 1
    dma = pltpu.SemaphoreType.DMA
    vmem = pl.BlockSpec(memory_space=pltpu.VMEM)
    smem = pl.BlockSpec(memory_space=pltpu.SMEM)
    anywhere = pl.BlockSpec(memory_space=pltpu.HBM)
    shapes = (
        jax.ShapeDtypeStruct(queries.shape, jnp.bfloat16),
        jax.ShapeDtypeStruct((1, tokens, kv_width), jnp.bfloat16),
    )
    landing = pl.pallas_call(
        functools.partial(kernel, sections, shards, groups, repeats),
        out_shape=tuple(pltpu.VMEM(x.shape, x.dtype) for x in shapes),
        in_specs=[anywhere] * 7,
        out_specs=(vmem, vmem),
        scratch_shapes=[
            pltpu.VMEM((tokens, queries.shape[2]), jnp.bfloat16),
            pltpu.VMEM((tokens, queries.shape[2]), jnp.bfloat16),
            pltpu.VMEM((2, groups, length, HEAD_DIM), jnp.bfloat16),
            pltpu.VMEM((2, groups, length, HEAD_DIM), jnp.bfloat16),
            pltpu.VMEM((groups, length, HEAD_DIM), jnp.bfloat16),
            pltpu.VMEM((groups, length, HEAD_DIM), jnp.bfloat16),
            pltpu.VMEM((groups, peers, tokens, HEAD_DIM), jnp.bfloat16),
            pltpu.VMEM((tokens, queries.shape[2]), jnp.bfloat16),
            pltpu.VMEM((tokens, kv_width), jnp.bfloat16),
            dma((groups, peers)), dma((groups, peers)),
            dma((groups, peers)), dma((groups, peers)),
            dma((groups,)), dma((groups,)),
            dma((groups, peers)), dma((groups, peers)),
            dma((groups, repeats)), dma((groups, repeats)),
            dma((groups,)), dma((groups,)),
            dma((2, groups)), dma((5,)),
            pltpu.SMEM(rand_blocks.T.shape, jnp.int32),
            pltpu.SMEM(global_blocks.shape, jnp.int32),
            pltpu.SMEM(win_reach.shape, jnp.int32),
        ],
        compiler_params=pltpu.CompilerParams(
            collective_id=0, has_side_effects=True, vmem_limit_bytes=62 * 1024 * 1024
        ),
    )(rand_blocks.T, global_blocks, win_reach, queries[0], out_grad[0], keys[0], values[0])
    pieces = 2
    return pl.pallas_call(
        functools.partial(copy_out, sections, pieces),
        out_shape=shapes,
        in_specs=[vmem, vmem],
        out_specs=(anywhere, anywhere),
        scratch_shapes=[
            pltpu.VMEM((tokens // pieces, queries.shape[2]), jnp.bfloat16),
            dma((2 * pieces,)),
        ],
    )(*(pltpu.with_memory_space_constraint(x, pltpu.VMEM) for x in landing))


def solution(mesh):
    placed = (
        P("section", "seq", "tp"),
        P("section", "seq", None),
        P("section", "seq", None),
        P("section", "seq", "tp"),
        P(),
        P(),
        P(),
    )
    return jax.shard_map(
        on_device,
        mesh=mesh,
        in_specs=placed,
        out_specs=(P("section", "seq", "tp"), P("section", "seq", "tp")),
        check_vma=False,
    )
```

```python
import functools
import math

import jax
import jax.numpy as jnp
from jax import lax
from jax.experimental import pallas as pl
from jax.experimental.pallas import tpu as pltpu
from jax.sharding import PartitionSpec as P

HEAD_DIM = 128
BLOCK_LEN = 64
WINDOW = 1
MESH = pl.DeviceIdType.MESH
NT = (((1,), (1,)), ((), ()))
TN = (((0,), (0,)), ((), ()))


def head_cols(h):
    return pl.ds(pl.multiple_of(h * HEAD_DIM, HEAD_DIM), HEAD_DIM)


def kernel(
    sections, shards, groups, repeats, rand_hbm, glob_hbm, reach_hbm,
    q_hbm, do_hbm, k_hbm, v_hbm, outq_ref, outkv_ref,
    q_ref, do_ref, kv_all, stage, sib, part, landed, dq, final,
    g_send, g_recv, f_send, f_recv, x_send, x_recv, r_send, r_recv,
    zq_send, zq_recv, zk_send, zk_recv, s_send, s_recv, own_sem, load_sem, table_sem,
    rand_ref, glob_ref, reach_ref,
):
    section = lax.axis_index("section")
    me = lax.axis_index("seq")
    t = lax.axis_index("tp")
    peers = shards - 1
    tokens = q_ref.shape[0]
    local_blocks = tokens // BLOCK_LEN
    all_blocks = local_blocks * shards
    scale = HEAD_DIM ** -0.5
    moved = groups - 1
    low = jnp.where(section > 0, 0, moved)
    high = jnp.where(section < sections - 1, groups, moved)

    def rows(shard):
        return pl.ds(pl.multiple_of(shard * tokens, tokens), tokens)

    def remote(src, dst, send, recv, device):
        return pltpu.make_async_remote_copy(
            src_ref=src, dst_ref=dst, send_sem=send, recv_sem=recv,
            device_id=device, device_id_type=MESH,
        )

    def own(half, g, source):
        return pltpu.make_async_copy(
            source.at[:, head_cols(g)], kv_all.at[half, g, rows(me)], own_sem.at[half, g]
        )

    def gather(g, d, shard, source=None):
        block = kv_all.at[t, g, rows(shard)]
        source = block if source is None else source.at[:, head_cols(g)]
        to = lax.rem(me + d, shards)
        return remote(source, block, g_send.at[g, d - 1], g_recv.at[g, d - 1], {"seq": to})

    def forward(g, d, half):
        block = kv_all.at[half, g, rows(lax.rem(me - d + shards, shards))]
        return remote(block, block, f_send.at[g, d], f_recv.at[g, d], {"tp": 1 - t})

    def exchange(g):
        return remote(stage.at[1 - t, g], sib.at[g], x_send.at[g], x_recv.at[g], {"tp": 1 - t})

    def scatter(g, d):
        to = lax.rem(me + d, shards)
        return remote(
            part.at[g, rows(to)], landed.at[g, d - 1],
            r_send.at[g, d - 1], r_recv.at[g, d - 1], {"seq": to},
        )

    def hand_query(g, r):
        cols = head_cols(r * groups + g)
        return remote(
            dq.at[:, cols], outq_ref.at[0, :, cols],
            zq_send.at[g, r], zq_recv.at[g, r], {"section": section - 1},
        )

    def hand_keyval(g):
        cols = head_cols(g)
        return remote(
            final.at[:, cols], outkv_ref.at[0, :, cols],
            zk_send.at[g], zk_recv.at[g], {"section": section - 1},
        )

    def hand_input(r, which):
        cols = head_cols(r * groups + moved)
        source, target = ((q_hbm, q_ref), (do_hbm, do_ref))[which]
        return remote(
            source.at[:, cols], target.at[:, cols],
            s_send.at[which, r], s_recv.at[which, r], {"section": section - 1},
        )

    def hand_shard(source):
        return remote(
            source.at[:, head_cols(moved)], kv_all.at[t, moved, rows(me)],
            s_send.at[2, 0], s_recv.at[2, 0], {"section": section - 1},
        )

    def load(r, which):
        cols = pl.ds(r * groups * HEAD_DIM, moved * HEAD_DIM)
        source, target = ((q_hbm, q_ref), (do_hbm, do_ref))[which]
        return pltpu.make_async_copy(source.at[:, cols], target.at[:, cols], load_sem.at[which, r])

    tables = [
        pltpu.make_async_copy(source, target, table_sem.at[i])
        for i, (source, target) in enumerate(
            ((rand_hbm, rand_ref), (glob_hbm, glob_ref), (reach_hbm, reach_ref))
        )
    ]
    for table in tables:
        table.start()

    @pl.when(section > 0)
    def _():
        @pl.loop(0, moved)
        def _(g):
            own(0, g, k_hbm).start()
            own(1, g, v_hbm).start()

        for r in range(repeats):
            load(r, 0).start()
            load(r, 1).start()

    barrier = pltpu.get_barrier_semaphore()

    @pl.loop(1, shards)
    def _(d):
        pl.semaphore_signal(
            barrier, inc=1, device_id={"seq": lax.rem(me + d, shards)}, device_id_type=MESH
        )

    pl.semaphore_signal(barrier, inc=1, device_id={"tp": 1 - t}, device_id_type=MESH)

    @pl.when(section < sections - 1)
    def _():
        pl.semaphore_signal(
            barrier, inc=1, device_id={"section": section + 1}, device_id_type=MESH
        )

    below = jnp.where(section > 0, 1, 0)
    pl.semaphore_wait(barrier, peers + 1 + below)

    @pl.when(section > 0)
    def _():
        for half, source in ((0, k_hbm), (1, v_hbm)):

            @pl.when(t == half)
            def _():
                hand_shard(source).start()

        for r in range(repeats):
            hand_input(r, 0).start()
            hand_input(r, 1).start()

    def spread(g):
        for half, source in ((0, k_hbm), (1, v_hbm)):

            @pl.when((g < moved) & (t == half))
            def _():
                @pl.loop(1, shards)
                def _(d):
                    gather(g, d, me, source).start()

        @pl.when(g == moved)
        def _():
            hand_shard(k_hbm).wait_recv()
            forward(g, 0, t).start()

            @pl.loop(1, shards)
            def _(d):
                gather(g, d, me).start()

    def sent(g):
        @pl.loop(1, shards)
        def _(d):
            gather(g, d, me).wait_send()

    def pass_on(g):
        @pl.loop(1, shards)
        def _(d):
            gather(g, d, lax.rem(me - d + shards, shards)).wait_recv()
            forward(g, d, t).start()

        @pl.when(g + 2 < high)
        def _():
            spread(g + 2)

    spread(low)
    sent(low)

    @pl.when(low + 1 < high)
    def _():
        spread(low + 1)

    def send_parts(g):
        exchange(g).wait_recv()
        both = stage[t, g].astype(jnp.float32) + sib[g].astype(jnp.float32)
        part[g] = both.astype(jnp.bfloat16)

        @pl.loop(1, shards)
        def _(d):
            scatter(g, d).start()

    for table in tables:
        table.wait()
    chunk = 2
    lag = 3
    width = chunk * tokens
    lane = lax.broadcasted_iota(jnp.int32, (all_blocks, width), 1)
    block_id = lax.broadcasted_iota(jnp.int32, (all_blocks, width), 0)
    lane_block = lax.rem(lane, tokens) // BLOCK_LEN
    lane_head = lane // tokens
    query_block = me * local_blocks + lane_block
    distance = jnp.abs(block_id - query_block)
    always = jnp.zeros((all_blocks, width), jnp.float32)
    for i in range(glob_ref.shape[0]):
        always += (block_id == glob_ref[i]).astype(jnp.float32)
    for i in range(rand_ref.shape[0]):
        for j in range(local_blocks):
            named = (lane_block == j) & (block_id == rand_ref[i, me * local_blocks + j])
            always += named.astype(jnp.float32)

    def finish(g):
        @pl.loop(1, shards)
        def _(d):
            scatter(g, d).wait_recv()

        total = part[g, rows(me), :].astype(jnp.float32)
        for d in range(1, shards):
            total += landed[g, d - 1].astype(jnp.float32)
        total = total.astype(jnp.bfloat16)

        @pl.when(g < moved)
        def _():
            final[:, head_cols(g)] = total
            hand_keyval(g).start()

        @pl.when(g == moved)
        def _():
            outkv_ref[0, :, head_cols(g)] = total

    pass_on(low)

    @pl.when(section > 0)
    def _():
        for r in range(repeats):
            load(r, 0).wait()
            load(r, 1).wait()

    @pl.loop(low, high)
    def _(g):
        @pl.when(g < moved)
        def _():
            own(0, g, k_hbm).wait()
            own(1, g, v_hbm).wait()

        @pl.when(g == moved)
        def _():
            forward(g, 0, 1 - t).wait_recv()
            for r in range(repeats):
                hand_input(r, 0).wait_recv()
                hand_input(r, 1).wait_recv()

        @pl.loop(1, shards)
        def _(d):
            forward(g, d, 1 - t).wait_recv()

        keys = kv_all[0, g]
        values = kv_all[1, g]
        key_grads = None
        for c in range(repeats // chunk):
            heads = [c * chunk + i for i in range(chunk)]
            query = jnp.concatenate([q_ref[:, head_cols(r * groups + g)] for r in heads], axis=0)
            grad = jnp.concatenate([do_ref[:, head_cols(r * groups + g)] for r in heads], axis=0)
            reach = jnp.zeros((all_blocks, width), jnp.int32)
            for i, r in enumerate(heads):
                reach = jnp.where(lane_head == i, reach_ref[(t * repeats + r) * groups + g], reach)
            window = (distance <= WINDOW) & (distance <= reach)
            count = always + window.astype(jnp.float32)
            bias = jnp.where(
                count > 0, jnp.log(jnp.maximum(count, 1.0)) * (1.0 / math.log(2.0)), -1e30
            )
            scores = lax.dot_general(keys, query, NT, preferred_element_type=jnp.float32)
            scores = scores.reshape(all_blocks, BLOCK_LEN, width) * (scale / math.log(2.0))
            scores = (scores + bias[:, None, :]).reshape(all_blocks * BLOCK_LEN, width)
            row_max = jnp.max(scores, axis=0, keepdims=True)
            terms = jnp.exp2(scores - row_max)
            weights = terms * (1.0 / jnp.sum(terms, axis=0, keepdims=True))
            weight_grads = lax.dot_general(values, grad, NT, preferred_element_type=jnp.float32)
            delta = jnp.sum(weights * weight_grads, axis=0, keepdims=True)
            grads_low = (weights * (weight_grads - delta)).astype(jnp.bfloat16)
            weights_low = weights.astype(jnp.bfloat16)
            query_grads = lax.dot_general(
                grads_low, keys, TN, preferred_element_type=jnp.float32
            )
            query_grads = (query_grads * scale).astype(jnp.bfloat16)

            @pl.when(g < moved)
            def _():
                for i, r in enumerate(heads):
                    dq[:, head_cols(r * groups + g)] = query_grads[i * tokens : (i + 1) * tokens]
                    hand_query(g, r).start()

            @pl.when(g == moved)
            def _():
                for i, r in enumerate(heads):
                    cols = head_cols(r * groups + g)
                    outq_ref[0, :, cols] = query_grads[i * tokens : (i + 1) * tokens]

            if c == 0:

                @pl.when(g + 1 < high)
                def _():
                    pass_on(g + 1)

            dk = jnp.dot(grads_low, query, preferred_element_type=jnp.float32)
            dv = jnp.dot(weights_low, grad, preferred_element_type=jnp.float32)
            key_grads = dk if key_grads is None else key_grads + dk
            value_grads = dv if c == 0 else value_grads + dv
        stage[0, g] = (key_grads * scale).astype(jnp.bfloat16)
        stage[1, g] = value_grads.astype(jnp.bfloat16)
        exchange(g).start()

        @pl.when(g > low)
        def _():
            send_parts(g - 1)

        @pl.when(g >= low + lag)
        def _():
            finish(g - lag)

    send_parts(high - 1)

    @pl.loop(lax.max(low, high - lag), high)
    def _(g):
        finish(g)

    @pl.loop(low + 1, high)
    def _(g):
        sent(g)

    @pl.loop(low, high)
    def _(g):
        @pl.loop(1, shards)
        def _(d):
            scatter(g, d).wait_send()
            forward(g, d, t).wait_send()

        exchange(g).wait_send()

    @pl.when(section > 0)
    def _():
        hand_shard(k_hbm).wait_send()
        for r in range(repeats):
            hand_input(r, 0).wait_send()
            hand_input(r, 1).wait_send()

        @pl.loop(0, moved)
        def _(g):
            for r in range(repeats):
                hand_query(g, r).wait_send()
            hand_keyval(g).wait_send()

    @pl.when(section < sections - 1)
    def _():
        forward(moved, 0, t).wait_send()

        @pl.loop(0, moved)
        def _(g):
            for r in range(repeats):
                hand_query(g, r).wait_recv()
            hand_keyval(g).wait_recv()


def copy_out(sections, pieces, q_in, kv_in, q_out, kv_out, blank, out_sem):
    section = lax.axis_index("section")
    size = q_in.shape[1] // pieces
    width = kv_in.shape[2]

    def stores(held):
        copies = []
        for k, (source, target) in enumerate(((q_in, q_out), (kv_in, kv_out))):
            for i in range(pieces):
                piece = pl.ds(i * size, size)
                src = source.at[0, piece] if held is None else held.at[:, pl.ds(0, source.shape[2])]
                copies.append(
                    pltpu.make_async_copy(src, target.at[0, piece], out_sem.at[k * pieces + i])
                )
        return copies

    @pl.when(section < sections - 1)
    def _():
        for store in stores(None):
            store.start()

    @pl.when(section == sections - 1)
    def _():
        blank[...] = jnp.zeros_like(blank)
        for store in stores(blank):
            store.start()

    for store in stores(None):
        store.wait()


def on_device(queries, keys, values, out_grad, rand_blocks, global_blocks, win_reach):
    sections = lax.axis_size("section")
    shards = lax.axis_size("seq")
    tokens = queries.shape[1]
    kv_width = keys.shape[2]
    groups = kv_width // HEAD_DIM
    repeats = queries.shape[2] // kv_width
    length = tokens * shards
    peers = shards - 1
    dma = pltpu.SemaphoreType.DMA
    vmem = pl.BlockSpec(memory_space=pltpu.VMEM)
    smem = pl.BlockSpec(memory_space=pltpu.SMEM)
    anywhere = pl.BlockSpec(memory_space=pltpu.HBM)
    shapes = (
        jax.ShapeDtypeStruct(queries.shape, jnp.bfloat16),
        jax.ShapeDtypeStruct((1, tokens, kv_width), jnp.bfloat16),
    )
    landing = pl.pallas_call(
        functools.partial(kernel, sections, shards, groups, repeats),
        out_shape=tuple(pltpu.VMEM(x.shape, x.dtype) for x in shapes),
        in_specs=[anywhere] * 7,
        out_specs=(vmem, vmem),
        scratch_shapes=[
            pltpu.VMEM((tokens, queries.shape[2]), jnp.bfloat16),
            pltpu.VMEM((tokens, queries.shape[2]), jnp.bfloat16),
            pltpu.VMEM((2, groups, length, HEAD_DIM), jnp.bfloat16),
            pltpu.VMEM((2, groups, length, HEAD_DIM), jnp.bfloat16),
            pltpu.VMEM((groups, length, HEAD_DIM), jnp.bfloat16),
            pltpu.VMEM((groups, length, HEAD_DIM), jnp.bfloat16),
            pltpu.VMEM((groups, peers, tokens, HEAD_DIM), jnp.bfloat16),
            pltpu.VMEM((tokens, queries.shape[2]), jnp.bfloat16),
            pltpu.VMEM((tokens, kv_width), jnp.bfloat16),
            dma((groups, peers)), dma((groups, peers)),
            dma((groups, shards)), dma((groups, shards)),
            dma((groups,)), dma((groups,)),
            dma((groups, peers)), dma((groups, peers)),
            dma((groups, repeats)), dma((groups, repeats)),
            dma((groups,)), dma((groups,)),
            dma((3, repeats)), dma((3, repeats)),
            dma((2, groups)), dma((2, repeats)), dma((3,)),
            pltpu.SMEM(rand_blocks.T.shape, jnp.int32),
            pltpu.SMEM(global_blocks.shape, jnp.int32),
            pltpu.SMEM(win_reach.shape, jnp.int32),
        ],
        compiler_params=pltpu.CompilerParams(
            collective_id=0, has_side_effects=True, vmem_limit_bytes=62 * 1024 * 1024
        ),
    )(rand_blocks.T, global_blocks, win_reach, queries[0], out_grad[0], keys[0], values[0])
    pieces = 2
    return pl.pallas_call(
        functools.partial(copy_out, sections, pieces),
        out_shape=shapes,
        in_specs=[vmem, vmem],
        out_specs=(anywhere, anywhere),
        scratch_shapes=[
            pltpu.VMEM((tokens // pieces, queries.shape[2]), jnp.bfloat16),
            dma((2 * pieces,)),
        ],
    )(*(pltpu.with_memory_space_constraint(x, pltpu.VMEM) for x in landing))


def solution(mesh):
    placed = (
        P("section", "seq", "tp"),
        P("section", "seq", None),
        P("section", "seq", None),
        P("section", "seq", "tp"),
        P(),
        P(),
        P(),
    )
    return jax.shard_map(
        on_device,
        mesh=mesh,
        in_specs=placed,
        out_specs=(P("section", "seq", "tp"), P("section", "seq", "tp")),
        check_vma=False,
    )
```

```python
import functools
import math

import jax
import jax.numpy as jnp
from jax import lax
from jax.experimental import pallas as pl
from jax.experimental.pallas import tpu as pltpu
from jax.sharding import PartitionSpec as P

HEAD_DIM = 128
BLOCK_LEN = 64
WINDOW = 1
MESH = pl.DeviceIdType.MESH
NT = (((1,), (1,)), ((), ()))
TN = (((0,), (0,)), ((), ()))


def head_cols(h):
    return pl.ds(pl.multiple_of(h * HEAD_DIM, HEAD_DIM), HEAD_DIM)


def kernel(
    sections, shards, groups, repeats, rand_hbm, glob_hbm, reach_hbm,
    q_hbm, do_hbm, k_hbm, v_hbm, outq_ref, outkv_ref,
    q_ref, do_ref, kv_all, stage, sib, part, landed, dq, final,
    g_send, g_recv, f_send, f0_send, f_recv, x_send, x_recv, r_send, r_recv,
    zq_send, zq_recv, zk_send, zk_recv, s_send, s_recv, own_sem, load_sem, table_sem,
    rand_ref, glob_ref, reach_ref,
):
    section = lax.axis_index("section")
    me = lax.axis_index("seq")
    t = lax.axis_index("tp")
    peers = shards - 1
    tokens = q_ref.shape[0]
    local_blocks = tokens // BLOCK_LEN
    all_blocks = local_blocks * shards
    scale = HEAD_DIM ** -0.5
    moved = groups - 1
    low = jnp.where(section > 0, 0, moved)
    high = jnp.where(section < sections - 1, groups, moved)

    def rows(shard):
        return pl.ds(pl.multiple_of(shard * tokens, tokens), tokens)

    def remote(src, dst, send, recv, device):
        return pltpu.make_async_remote_copy(
            src_ref=src, dst_ref=dst, send_sem=send, recv_sem=recv,
            device_id=device, device_id_type=MESH,
        )

    def own(half, g, source):
        return pltpu.make_async_copy(
            source.at[:, head_cols(g)], kv_all.at[half, g, rows(me)], own_sem
        )

    def gather(g, d, shard, source=None):
        block = kv_all.at[t, g, rows(shard)]
        source = block if source is None else source.at[:, head_cols(g)]
        to = lax.rem(me + d, shards)
        return remote(source, block, g_send.at[jnp.where(g == low, 0, 1)], g_recv.at[g], {"seq": to})

    def forward(g, d, half):
        block = kv_all.at[half, g, rows(lax.rem(me - d + shards, shards))]
        return remote(block, block, f_send, f_recv.at[g], {"tp": 1 - t})

    def exchange(g):
        return remote(stage.at[1 - t, g], sib.at[g], x_send, x_recv.at[g], {"tp": 1 - t})

    def scatter(g, d):
        to = lax.rem(me + d, shards)
        return remote(
            part.at[g, rows(to)], landed.at[g, d - 1],
            r_send, r_recv.at[g], {"seq": to},
        )

    def hand_query(g, r):
        cols = head_cols(r * groups + g)
        return remote(
            dq.at[:, cols], outq_ref.at[0, :, cols],
            zq_send, zq_recv, {"section": section - 1},
        )

    def hand_keyval(g):
        cols = head_cols(g)
        return remote(
            final.at[:, cols], outkv_ref.at[0, :, cols],
            zk_send, zk_recv, {"section": section - 1},
        )

    def hand_input(r, which):
        cols = head_cols(r * groups + moved)
        source, target = ((q_hbm, q_ref), (do_hbm, do_ref))[which]
        return remote(
            source.at[:, cols], target.at[:, cols],
            s_send, s_recv.at[0], {"section": section - 1},
        )

    def hand_shard(source):
        return remote(
            source.at[:, head_cols(moved)], kv_all.at[t, moved, rows(me)],
            s_send, s_recv.at[1], {"section": section - 1},
        )

    def load(r, which):
        cols = pl.ds(r * groups * HEAD_DIM, moved * HEAD_DIM)
        source, target = ((q_hbm, q_ref), (do_hbm, do_ref))[which]
        return pltpu.make_async_copy(source.at[:, cols], target.at[:, cols], load_sem.at[which])

    def arrived(sem, ref):
        remote(ref, ref, sem, sem, {"tp": 1 - t}).wait_recv()

    def left(sem, ref):
        remote(ref, ref, sem, sem, {"tp": 1 - t}).wait_send()

    def loaded(sem, ref):
        pltpu.make_async_copy(ref, ref, sem).wait()

    def pieces(count):
        return kv_all.at[0, pl.ds(0, count), pl.ds(0, peers * tokens)]

    tables = [
        pltpu.make_async_copy(source, target, table_sem.at[i])
        for i, (source, target) in enumerate(
            ((rand_hbm, rand_ref), (glob_hbm, glob_ref), (reach_hbm, reach_ref))
        )
    ]
    barrier = pltpu.get_barrier_semaphore()

    @pl.loop(1, shards)
    def _(d):
        pl.semaphore_signal(
            barrier, inc=1, device_id={"seq": lax.rem(me + d, shards)}, device_id_type=MESH
        )

    pl.semaphore_signal(barrier, inc=1, device_id={"tp": 1 - t}, device_id_type=MESH)

    @pl.when(section < sections - 1)
    def _():
        pl.semaphore_signal(
            barrier, inc=1, device_id={"section": section + 1}, device_id_type=MESH
        )

    for table in tables:
        table.start()

    @pl.when(section > 0)
    def _():
        @pl.loop(0, moved)
        def _(g):
            own(0, g, k_hbm).start()
            own(1, g, v_hbm).start()

        for r in range(repeats):
            load(r, 0).start()
            load(r, 1).start()

    below = jnp.where(section > 0, 1, 0)
    pl.semaphore_wait(barrier, peers + 1 + below)

    @pl.when(section > 0)
    def _():
        for half, source in ((0, k_hbm), (1, v_hbm)):

            @pl.when(t == half)
            def _():
                hand_shard(source).start()

        for r in range(repeats):
            hand_input(r, 0).start()
            hand_input(r, 1).start()

    def spread(g):
        for half, source in ((0, k_hbm), (1, v_hbm)):

            @pl.when((g < moved) & (t == half))
            def _():
                @pl.loop(1, shards)
                def _(d):
                    gather(g, d, me, source).start()

        @pl.when(g == moved)
        def _():
            arrived(s_recv.at[1], kv_all.at[t, moved, rows(me)])
            block = kv_all.at[t, g, rows(me)]
            remote(block, block, f0_send, f_recv.at[g], {"tp": 1 - t}).start()

            @pl.loop(1, shards)
            def _(d):
                gather(g, d, me).start()

    def pass_on(g):
        arrived(g_recv.at[g], pieces(1))

        @pl.loop(1, shards)
        def _(d):
            forward(g, d, t).start()

        @pl.when(g + 2 < high)
        def _():
            spread(g + 2)

    spread(low)
    left(g_send.at[0], pieces(1))

    @pl.when(low + 1 < high)
    def _():
        spread(low + 1)

    def send_parts(g):
        arrived(x_recv.at[g], sib.at[g])
        both = stage[t, g].astype(jnp.float32) + sib[g].astype(jnp.float32)
        part[g] = both.astype(jnp.bfloat16)

        @pl.loop(1, shards)
        def _(d):
            scatter(g, d).start()

    for table in tables:
        table.wait()
    chunk = 2
    lag = 3
    width = chunk * tokens
    lane = lax.broadcasted_iota(jnp.int32, (all_blocks, width), 1)
    block_id = lax.broadcasted_iota(jnp.int32, (all_blocks, width), 0)
    lane_block = lax.rem(lane, tokens) // BLOCK_LEN
    lane_head = lane // tokens
    query_block = me * local_blocks + lane_block
    distance = jnp.abs(block_id - query_block)
    always = jnp.zeros((all_blocks, width), jnp.float32)
    for i in range(glob_ref.shape[0]):
        always += (block_id == glob_ref[i]).astype(jnp.float32)
    for i in range(rand_ref.shape[0]):
        for j in range(local_blocks):
            named = (lane_block == j) & (block_id == rand_ref[i, me * local_blocks + j])
            always += named.astype(jnp.float32)

    def finish(g):
        arrived(r_recv.at[g], landed.at[g])
        total = part[g, rows(me), :].astype(jnp.float32)
        for d in range(1, shards):
            total += landed[g, d - 1].astype(jnp.float32)
        total = total.astype(jnp.bfloat16)

        @pl.when(g < moved)
        def _():
            final[:, head_cols(g)] = total
            hand_keyval(g).start()

        @pl.when(g == moved)
        def _():
            outkv_ref[0, :, head_cols(g)] = total

    pass_on(low)

    own_width = repeats * moved * HEAD_DIM

    @pl.when(section > 0)
    def _():
        loaded(load_sem.at[0], q_ref.at[:, pl.ds(0, own_width)])
        loaded(load_sem.at[1], do_ref.at[:, pl.ds(0, own_width)])
        loaded(own_sem, dq.at[:, pl.ds(0, 2 * moved * HEAD_DIM)])

    @pl.loop(low, high)
    def _(g):
        @pl.when(g < moved)
        def _():
            arrived(f_recv.at[g], pieces(1))

        @pl.when(g == moved)
        def _():
            arrived(f_recv.at[g], kv_all.at[0, g])
            arrived(s_recv.at[0], q_ref.at[:, pl.ds(0, 2 * repeats * HEAD_DIM)])

        keys = kv_all[0, g]
        values = kv_all[1, g]
        key_grads = None
        for c in range(repeats // chunk):
            heads = [c * chunk + i for i in range(chunk)]
            query = jnp.concatenate([q_ref[:, head_cols(r * groups + g)] for r in heads], axis=0)
            grad = jnp.concatenate([do_ref[:, head_cols(r * groups + g)] for r in heads], axis=0)
            reach = jnp.zeros((all_blocks, width), jnp.int32)
            for i, r in enumerate(heads):
                reach = jnp.where(lane_head == i, reach_ref[(t * repeats + r) * groups + g], reach)
            window = (distance <= WINDOW) & (distance <= reach)
            count = always + window.astype(jnp.float32)
            bias = jnp.where(
                count > 0, jnp.log(jnp.maximum(count, 1.0)) * (1.0 / math.log(2.0)), -1e30
            )
            scores = lax.dot_general(keys, query, NT, preferred_element_type=jnp.float32)
            scores = scores.reshape(all_blocks, BLOCK_LEN, width) * (scale / math.log(2.0))
            scores = (scores + bias[:, None, :]).reshape(all_blocks * BLOCK_LEN, width)
            row_max = jnp.max(scores, axis=0, keepdims=True)
            terms = jnp.exp2(scores - row_max)
            weights = terms * (1.0 / jnp.sum(terms, axis=0, keepdims=True))
            weight_grads = lax.dot_general(values, grad, NT, preferred_element_type=jnp.float32)
            delta = jnp.sum(weights * weight_grads, axis=0, keepdims=True)
            grads_low = (weights * (weight_grads - delta)).astype(jnp.bfloat16)
            weights_low = weights.astype(jnp.bfloat16)
            query_grads = lax.dot_general(
                grads_low, keys, TN, preferred_element_type=jnp.float32
            )
            query_grads = (query_grads * scale).astype(jnp.bfloat16)

            @pl.when(g < moved)
            def _():
                for i, r in enumerate(heads):
                    dq[:, head_cols(r * groups + g)] = query_grads[i * tokens : (i + 1) * tokens]
                    hand_query(g, r).start()

            @pl.when(g == moved)
            def _():
                for i, r in enumerate(heads):
                    cols = head_cols(r * groups + g)
                    outq_ref[0, :, cols] = query_grads[i * tokens : (i + 1) * tokens]

            if c == 0:

                @pl.when(g + 1 < high)
                def _():
                    pass_on(g + 1)

            dk = jnp.dot(grads_low, query, preferred_element_type=jnp.float32)
            dv = jnp.dot(weights_low, grad, preferred_element_type=jnp.float32)
            key_grads = dk if key_grads is None else key_grads + dk
            value_grads = dv if c == 0 else value_grads + dv
        stage[0, g] = (key_grads * scale).astype(jnp.bfloat16)
        stage[1, g] = value_grads.astype(jnp.bfloat16)
        exchange(g).start()

        @pl.when(g > low)
        def _():
            send_parts(g - 1)

        @pl.when(g >= low + lag)
        def _():
            finish(g - lag)

    send_parts(high - 1)

    @pl.loop(lax.max(low, high - lag), high)
    def _(g):
        finish(g)

    for count, some in (
        (1, section == 0),
        (groups - 1, section == sections - 1),
        (groups, (section > 0) & (section < sections - 1)),
    ):

        @pl.when(some)
        def _():
            if count > 1:
                left(g_send.at[1], pieces(count - 1))
            left(f_send, pieces(count))
            left(r_send, pieces(count))
            left(x_send, sib.at[pl.ds(0, count)])

    @pl.when(section > 0)
    def _():
        left(s_send, q_ref.at[:, pl.ds(0, (2 * repeats + 1) * HEAD_DIM)])
        left(zq_send, dq.at[:, pl.ds(0, own_width)])
        left(zk_send, final.at[:, pl.ds(0, moved * HEAD_DIM)])

    @pl.when(section < sections - 1)
    def _():
        left(f0_send, kv_all.at[t, moved, rows(me)])
        arrived(zq_recv, outq_ref.at[0, :, pl.ds(0, own_width)])
        arrived(zk_recv, outkv_ref.at[0, :, pl.ds(0, moved * HEAD_DIM)])


def copy_out(sections, pieces, q_in, kv_in, q_out, kv_out, blank, out_sem):
    section = lax.axis_index("section")
    size = q_in.shape[1] // pieces
    width = kv_in.shape[2]

    def stores(held):
        copies = []
        for k, (source, target) in enumerate(((q_in, q_out), (kv_in, kv_out))):
            for i in range(pieces):
                piece = pl.ds(i * size, size)
                src = source.at[0, piece] if held is None else held.at[:, pl.ds(0, source.shape[2])]
                copies.append(
                    pltpu.make_async_copy(src, target.at[0, piece], out_sem.at[k * pieces + i])
                )
        return copies

    @pl.when(section < sections - 1)
    def _():
        for store in stores(None):
            store.start()

    @pl.when(section == sections - 1)
    def _():
        blank[...] = jnp.zeros_like(blank)
        for store in stores(blank):
            store.start()

    for store in stores(None):
        store.wait()


def on_device(queries, keys, values, out_grad, rand_blocks, global_blocks, win_reach):
    sections = lax.axis_size("section")
    shards = lax.axis_size("seq")
    tokens = queries.shape[1]
    kv_width = keys.shape[2]
    groups = kv_width // HEAD_DIM
    repeats = queries.shape[2] // kv_width
    length = tokens * shards
    peers = shards - 1
    dma = pltpu.SemaphoreType.DMA
    vmem = pl.BlockSpec(memory_space=pltpu.VMEM)
    smem = pl.BlockSpec(memory_space=pltpu.SMEM)
    anywhere = pl.BlockSpec(memory_space=pltpu.HBM)
    shapes = (
        jax.ShapeDtypeStruct(queries.shape, jnp.bfloat16),
        jax.ShapeDtypeStruct((1, tokens, kv_width), jnp.bfloat16),
    )
    landing = pl.pallas_call(
        functools.partial(kernel, sections, shards, groups, repeats),
        out_shape=tuple(pltpu.VMEM(x.shape, x.dtype) for x in shapes),
        in_specs=[anywhere] * 7,
        out_specs=(vmem, vmem),
        scratch_shapes=[
            pltpu.VMEM((tokens, queries.shape[2]), jnp.bfloat16),
            pltpu.VMEM((tokens, queries.shape[2]), jnp.bfloat16),
            pltpu.VMEM((2, groups, length, HEAD_DIM), jnp.bfloat16),
            pltpu.VMEM((2, groups, length, HEAD_DIM), jnp.bfloat16),
            pltpu.VMEM((groups, length, HEAD_DIM), jnp.bfloat16),
            pltpu.VMEM((groups, length, HEAD_DIM), jnp.bfloat16),
            pltpu.VMEM((groups, peers, tokens, HEAD_DIM), jnp.bfloat16),
            pltpu.VMEM((tokens, queries.shape[2]), jnp.bfloat16),
            pltpu.VMEM((tokens, kv_width), jnp.bfloat16),
            dma((2,)), dma((groups,)),
            dma, dma, dma((groups,)),
            dma, dma((groups,)),
            dma, dma((groups,)),
            dma, dma, dma, dma,
            dma, dma((2,)),
            dma, dma((2,)), dma((3,)),
            pltpu.SMEM(rand_blocks.T.shape, jnp.int32),
            pltpu.SMEM(global_blocks.shape, jnp.int32),
            pltpu.SMEM(win_reach.shape, jnp.int32),
        ],
        compiler_params=pltpu.CompilerParams(
            collective_id=0, has_side_effects=True, vmem_limit_bytes=62 * 1024 * 1024
        ),
    )(rand_blocks.T, global_blocks, win_reach, queries[0], out_grad[0], keys[0], values[0])
    pieces = 2
    return pl.pallas_call(
        functools.partial(copy_out, sections, pieces),
        out_shape=shapes,
        in_specs=[vmem, vmem],
        out_specs=(anywhere, anywhere),
        scratch_shapes=[
            pltpu.VMEM((tokens // pieces, queries.shape[2]), jnp.bfloat16),
            dma((2 * pieces,)),
        ],
    )(*(pltpu.with_memory_space_constraint(x, pltpu.VMEM) for x in landing))


def solution(mesh):
    placed = (
        P("section", "seq", "tp"),
        P("section", "seq", None),
        P("section", "seq", None),
        P("section", "seq", "tp"),
        P(),
        P(),
        P(),
    )
    return jax.shard_map(
        on_device,
        mesh=mesh,
        in_specs=placed,
        out_specs=(P("section", "seq", "tp"), P("section", "seq", "tp")),
        check_vma=False,
    )
```

```python
import functools
import math

import jax
import jax.numpy as jnp
from jax import lax
from jax.experimental import pallas as pl
from jax.experimental.pallas import tpu as pltpu
from jax.sharding import PartitionSpec as P

HEAD_DIM = 128
BLOCK_LEN = 64
WINDOW = 1
MESH = pl.DeviceIdType.MESH
NT = (((1,), (1,)), ((), ()))
TN = (((0,), (0,)), ((), ()))


DETOUR = 2
DETOUR_GROUP = 2


def head_cols(h):
    return pl.ds(pl.multiple_of(h * HEAD_DIM, HEAD_DIM), HEAD_DIM)


def kernel(
    sections, shards, groups, repeats, rand_hbm, glob_hbm, reach_hbm,
    q_hbm, do_hbm, k_hbm, v_hbm, outq_ref, outkv_ref,
    q_ref, do_ref, kv_all, stage, sib, part, landed, dq, final,
    g_send, g_recv, f_send, f0_send, f_recv, x_send, x_recv, r_send, r_recv,
    zq_send, zq_recv, zk_send, zk_recv, s_send, s_recv, own_sem, load_sem, table_sem,
    rand_ref, glob_ref, reach_ref, hop, hop_send, hop_recv,
):
    section = lax.axis_index("section")
    me = lax.axis_index("seq")
    t = lax.axis_index("tp")
    peers = shards - 1
    tokens = q_ref.shape[0]
    local_blocks = tokens // BLOCK_LEN
    all_blocks = local_blocks * shards
    scale = HEAD_DIM ** -0.5
    moved = groups - 1
    detours = DETOUR if shards > DETOUR and repeats > DETOUR else 0
    helps = (me > 0) & (me <= detours)
    low = jnp.where(section > 0, 0, moved)
    high = jnp.where(section < sections - 1, groups, moved)

    def rows(shard):
        return pl.ds(pl.multiple_of(shard * tokens, tokens), tokens)

    def remote(src, dst, send, recv, device):
        return pltpu.make_async_remote_copy(
            src_ref=src, dst_ref=dst, send_sem=send, recv_sem=recv,
            device_id=device, device_id_type=MESH,
        )

    def own(half, g, source):
        return pltpu.make_async_copy(
            source.at[:, head_cols(g)], kv_all.at[half, g, rows(me)], own_sem
        )

    def gather(g, d, shard, source=None):
        block = kv_all.at[t, g, rows(shard)]
        source = block if source is None else source.at[:, head_cols(g)]
        to = lax.rem(me + d, shards)
        return remote(source, block, g_send.at[jnp.where(g == low, 0, 1)], g_recv.at[g], {"seq": to})

    def forward(g, d, half):
        block = kv_all.at[half, g, rows(lax.rem(me - d + shards, shards))]
        return remote(block, block, f_send, f_recv.at[g], {"tp": 1 - t})

    def exchange(g):
        return remote(stage.at[1 - t, g], sib.at[g], x_send, x_recv.at[g], {"tp": 1 - t})

    def scatter(g, d):
        to = lax.rem(me + d, shards)
        return remote(
            part.at[g, rows(to)], landed.at[g, d - 1],
            r_send, r_recv.at[g], {"seq": to},
        )

    def hand_query(g, r):
        cols = head_cols(r * groups + g)
        return remote(
            dq.at[:, cols], outq_ref.at[0, :, cols],
            zq_send, zq_recv, {"section": section - 1},
        )

    def detour(r):
        return remote(
            dq.at[:, head_cols(r * groups + DETOUR_GROUP)], hop,
            zq_send, hop_recv, {"seq": r + 1},
        )

    def hand_on():
        cols = head_cols((me - 1) * groups + DETOUR_GROUP)
        return remote(
            hop, outq_ref.at[0, :, cols], hop_send, zq_recv,
            {"section": section - 1, "seq": 0},
        )

    def hand_keyval(g):
        cols = head_cols(g)
        return remote(
            final.at[:, cols], outkv_ref.at[0, :, cols],
            zk_send, zk_recv, {"section": section - 1},
        )

    def hand_input(r, which):
        cols = head_cols(r * groups + moved)
        source, target = ((q_hbm, q_ref), (do_hbm, do_ref))[which]
        return remote(
            source.at[:, cols], target.at[:, cols],
            s_send, s_recv.at[0], {"section": section - 1},
        )

    def hand_shard(source):
        return remote(
            source.at[:, head_cols(moved)], kv_all.at[t, moved, rows(me)],
            s_send, s_recv.at[1], {"section": section - 1},
        )

    def load(r, which):
        cols = pl.ds(r * groups * HEAD_DIM, moved * HEAD_DIM)
        source, target = ((q_hbm, q_ref), (do_hbm, do_ref))[which]
        return pltpu.make_async_copy(source.at[:, cols], target.at[:, cols], load_sem.at[which])

    def arrived(sem, ref):
        remote(ref, ref, sem, sem, {"tp": 1 - t}).wait_recv()

    def left(sem, ref):
        remote(ref, ref, sem, sem, {"tp": 1 - t}).wait_send()

    def loaded(sem, ref):
        pltpu.make_async_copy(ref, ref, sem).wait()

    def pieces(count):
        return kv_all.at[0, pl.ds(0, count), pl.ds(0, peers * tokens)]

    tables = [
        pltpu.make_async_copy(source, target, table_sem.at[i])
        for i, (source, target) in enumerate(
            ((rand_hbm, rand_ref), (glob_hbm, glob_ref), (reach_hbm, reach_ref))
        )
    ]
    barrier = pltpu.get_barrier_semaphore()

    @pl.loop(1, shards)
    def _(d):
        pl.semaphore_signal(
            barrier, inc=1, device_id={"seq": lax.rem(me + d, shards)}, device_id_type=MESH
        )

    pl.semaphore_signal(barrier, inc=1, device_id={"tp": 1 - t}, device_id_type=MESH)

    @pl.when(section < sections - 1)
    def _():
        pl.semaphore_signal(
            barrier, inc=1, device_id={"section": section + 1}, device_id_type=MESH
        )

        @pl.when(me == 0)
        def _():
            for r in range(detours):
                pl.semaphore_signal(
                    barrier, inc=1, device_id={"section": section + 1, "seq": r + 1},
                    device_id_type=MESH,
                )

    for table in tables:
        table.start()

    below = jnp.where(section > 0, 1 + jnp.where(helps, 1, 0), 0)
    pl.semaphore_wait(barrier, peers + 1 + below)

    @pl.when(section > 0)
    def _():
        for half, source in ((0, k_hbm), (1, v_hbm)):

            @pl.when(t == half)
            def _():
                hand_shard(source).start()

    def spread(g):
        for half, source in ((0, k_hbm), (1, v_hbm)):

            @pl.when((g < moved) & (t == half))
            def _():
                @pl.loop(1, shards)
                def _(d):
                    gather(g, d, me, source).start()

        @pl.when(g == moved)
        def _():
            arrived(s_recv.at[1], kv_all.at[t, moved, rows(me)])
            block = kv_all.at[t, g, rows(me)]
            remote(block, block, f0_send, f_recv.at[g], {"tp": 1 - t}).start()

            @pl.loop(1, shards)
            def _(d):
                gather(g, d, me).start()

    def pass_on(g):
        arrived(g_recv.at[g], pieces(1))

        @pl.loop(1, shards)
        def _(d):
            forward(g, d, t).start()

        @pl.when(g + 2 < high)
        def _():
            spread(g + 2)

    spread(low)

    @pl.when(section > 0)
    def _():
        for r in range(repeats):
            hand_input(r, 0).start()
            hand_input(r, 1).start()

    @pl.when(section > 0)
    def _():
        @pl.loop(0, moved)
        def _(g):
            own(0, g, k_hbm).start()
            own(1, g, v_hbm).start()

        for r in range(repeats):
            load(r, 0).start()
            load(r, 1).start()

    left(g_send.at[0], pieces(1))

    @pl.when(low + 1 < high)
    def _():
        spread(low + 1)

    def send_parts(g):
        arrived(x_recv.at[g], sib.at[g])
        both = stage[t, g].astype(jnp.float32) + sib[g].astype(jnp.float32)
        part[g] = both.astype(jnp.bfloat16)

        @pl.loop(1, shards)
        def _(d):
            scatter(g, d).start()

    for table in tables:
        table.wait()
    chunk = 2
    lag = 3
    width = chunk * tokens
    lane = lax.broadcasted_iota(jnp.int32, (all_blocks, width), 1)
    block_id = lax.broadcasted_iota(jnp.int32, (all_blocks, width), 0)
    lane_block = lax.rem(lane, tokens) // BLOCK_LEN
    lane_head = lane // tokens
    query_block = me * local_blocks + lane_block
    distance = jnp.abs(block_id - query_block)
    always = jnp.zeros((all_blocks, width), jnp.float32)
    for i in range(glob_ref.shape[0]):
        always += (block_id == glob_ref[i]).astype(jnp.float32)
    for i in range(rand_ref.shape[0]):
        for j in range(local_blocks):
            named = (lane_block == j) & (block_id == rand_ref[i, me * local_blocks + j])
            always += named.astype(jnp.float32)

    def finish(g):
        arrived(r_recv.at[g], landed.at[g])
        total = part[g, rows(me), :].astype(jnp.float32)
        for d in range(1, shards):
            total += landed[g, d - 1].astype(jnp.float32)
        total = total.astype(jnp.bfloat16)

        @pl.when(g < moved)
        def _():
            final[:, head_cols(g)] = total
            hand_keyval(g).start()

        @pl.when(g == moved)
        def _():
            outkv_ref[0, :, head_cols(g)] = total

    pass_on(low)

    own_width = repeats * moved * HEAD_DIM

    @pl.when(section > 0)
    def _():
        loaded(load_sem.at[0], q_ref.at[:, pl.ds(0, own_width)])
        loaded(load_sem.at[1], do_ref.at[:, pl.ds(0, own_width)])
        loaded(own_sem, dq.at[:, pl.ds(0, 2 * moved * HEAD_DIM)])

    @pl.loop(low, high)
    def _(g):
        @pl.when(g < moved)
        def _():
            arrived(f_recv.at[g], pieces(1))

        @pl.when(g == moved)
        def _():
            arrived(f_recv.at[g], kv_all.at[0, g])
            arrived(s_recv.at[0], q_ref.at[:, pl.ds(0, 2 * repeats * HEAD_DIM)])

        keys = kv_all[0, g]
        values = kv_all[1, g]
        key_grads = None
        for c in range(repeats // chunk):
            heads = [c * chunk + i for i in range(chunk)]
            query = jnp.concatenate([q_ref[:, head_cols(r * groups + g)] for r in heads], axis=0)
            grad = jnp.concatenate([do_ref[:, head_cols(r * groups + g)] for r in heads], axis=0)
            reach = jnp.zeros((all_blocks, width), jnp.int32)
            for i, r in enumerate(heads):
                reach = jnp.where(lane_head == i, reach_ref[(t * repeats + r) * groups + g], reach)
            window = (distance <= WINDOW) & (distance <= reach)
            count = always + window.astype(jnp.float32)
            bias = jnp.where(
                count > 0, jnp.log(jnp.maximum(count, 1.0)) * (1.0 / math.log(2.0)), -1e30
            )
            scores = lax.dot_general(keys, query, NT, preferred_element_type=jnp.float32)
            scores = scores.reshape(all_blocks, BLOCK_LEN, width) * (scale / math.log(2.0))
            scores = (scores + bias[:, None, :]).reshape(all_blocks * BLOCK_LEN, width)
            row_max = jnp.max(scores, axis=0, keepdims=True)
            terms = jnp.exp2(scores - row_max)
            weights = terms * (1.0 / jnp.sum(terms, axis=0, keepdims=True))
            weight_grads = lax.dot_general(values, grad, NT, preferred_element_type=jnp.float32)
            delta = jnp.sum(weights * weight_grads, axis=0, keepdims=True)
            grads_low = (weights * (weight_grads - delta)).astype(jnp.bfloat16)
            weights_low = weights.astype(jnp.bfloat16)
            query_grads = lax.dot_general(
                grads_low, keys, TN, preferred_element_type=jnp.float32
            )
            query_grads = (query_grads * scale).astype(jnp.bfloat16)

            @pl.when(g < moved)
            def _():
                for i, r in enumerate(heads):
                    dq[:, head_cols(r * groups + g)] = query_grads[i * tokens : (i + 1) * tokens]
                    if r >= detours:
                        hand_query(g, r).start()
                    else:
                        around = (g == DETOUR_GROUP) & (me == 0)

                        @pl.when(around)
                        def _():
                            detour(r).start()

                        @pl.when(jnp.logical_not(around))
                        def _():
                            hand_query(g, r).start()

            @pl.when(g == moved)
            def _():
                for i, r in enumerate(heads):
                    cols = head_cols(r * groups + g)
                    outq_ref[0, :, cols] = query_grads[i * tokens : (i + 1) * tokens]

            if c == 0:

                @pl.when(g + 1 < high)
                def _():
                    pass_on(g + 1)

            dk = jnp.dot(grads_low, query, preferred_element_type=jnp.float32)
            dv = jnp.dot(weights_low, grad, preferred_element_type=jnp.float32)
            key_grads = dk if key_grads is None else key_grads + dk
            value_grads = dv if c == 0 else value_grads + dv
        stage[0, g] = (key_grads * scale).astype(jnp.bfloat16)
        stage[1, g] = value_grads.astype(jnp.bfloat16)
        exchange(g).start()

        @pl.when(g > low)
        def _():
            send_parts(g - 1)

        @pl.when(g >= low + lag)
        def _():
            finish(g - lag)

        @pl.when((g == DETOUR_GROUP + 1) & helps)
        def _():
            arrived(hop_recv, hop)
            hand_on().start()

    send_parts(high - 1)

    @pl.loop(lax.max(low, high - lag), high)
    def _(g):
        finish(g)

    for count, some in (
        (1, section == 0),
        (groups - 1, section == sections - 1),
        (groups, (section > 0) & (section < sections - 1)),
    ):

        @pl.when(some)
        def _():
            if count > 1:
                left(g_send.at[1], pieces(count - 1))
            left(f_send, pieces(count))
            left(r_send, pieces(count))
            left(x_send, sib.at[pl.ds(0, count)])

    @pl.when(section > 0)
    def _():
        left(s_send, q_ref.at[:, pl.ds(0, (2 * repeats + 1) * HEAD_DIM)])
        left(zq_send, dq.at[:, pl.ds(0, own_width)])

        @pl.when(helps)
        def _():
            left(hop_send, hop)

        left(zk_send, final.at[:, pl.ds(0, moved * HEAD_DIM)])

    @pl.when(section < sections - 1)
    def _():
        left(f0_send, kv_all.at[t, moved, rows(me)])
        arrived(zq_recv, outq_ref.at[0, :, pl.ds(0, own_width)])
        arrived(zk_recv, outkv_ref.at[0, :, pl.ds(0, moved * HEAD_DIM)])


def copy_out(sections, pieces, q_in, kv_in, q_out, kv_out, blank, out_sem):
    section = lax.axis_index("section")
    size = q_in.shape[1] // pieces
    width = kv_in.shape[2]

    def stores(held):
        copies = []
        for k, (source, target) in enumerate(((q_in, q_out), (kv_in, kv_out))):
            for i in range(pieces):
                piece = pl.ds(i * size, size)
                src = source.at[0, piece] if held is None else held.at[:, pl.ds(0, source.shape[2])]
                copies.append(
                    pltpu.make_async_copy(src, target.at[0, piece], out_sem.at[k * pieces + i])
                )
        return copies

    @pl.when(section < sections - 1)
    def _():
        for store in stores(None):
            store.start()

    @pl.when(section == sections - 1)
    def _():
        blank[...] = jnp.zeros_like(blank)
        for store in stores(blank):
            store.start()

    for store in stores(None):
        store.wait()


def on_device(queries, keys, values, out_grad, rand_blocks, global_blocks, win_reach):
    sections = lax.axis_size("section")
    shards = lax.axis_size("seq")
    tokens = queries.shape[1]
    kv_width = keys.shape[2]
    groups = kv_width // HEAD_DIM
    repeats = queries.shape[2] // kv_width
    length = tokens * shards
    peers = shards - 1
    dma = pltpu.SemaphoreType.DMA
    vmem = pl.BlockSpec(memory_space=pltpu.VMEM)
    smem = pl.BlockSpec(memory_space=pltpu.SMEM)
    anywhere = pl.BlockSpec(memory_space=pltpu.HBM)
    shapes = (
        jax.ShapeDtypeStruct(queries.shape, jnp.bfloat16),
        jax.ShapeDtypeStruct((1, tokens, kv_width), jnp.bfloat16),
    )
    landing = pl.pallas_call(
        functools.partial(kernel, sections, shards, groups, repeats),
        out_shape=tuple(pltpu.VMEM(x.shape, x.dtype) for x in shapes),
        in_specs=[anywhere] * 7,
        out_specs=(vmem, vmem),
        scratch_shapes=[
            pltpu.VMEM((tokens, queries.shape[2]), jnp.bfloat16),
            pltpu.VMEM((tokens, queries.shape[2]), jnp.bfloat16),
            pltpu.VMEM((2, groups, length, HEAD_DIM), jnp.bfloat16),
            pltpu.VMEM((2, groups, length, HEAD_DIM), jnp.bfloat16),
            pltpu.VMEM((groups, length, HEAD_DIM), jnp.bfloat16),
            pltpu.VMEM((groups, length, HEAD_DIM), jnp.bfloat16),
            pltpu.VMEM((groups, peers, tokens, HEAD_DIM), jnp.bfloat16),
            pltpu.VMEM((tokens, queries.shape[2]), jnp.bfloat16),
            pltpu.VMEM((tokens, kv_width), jnp.bfloat16),
            dma((2,)), dma((groups,)),
            dma, dma, dma((groups,)),
            dma, dma((groups,)),
            dma, dma((groups,)),
            dma, dma, dma, dma,
            dma, dma((2,)),
            dma, dma((2,)), dma((3,)),
            pltpu.SMEM(rand_blocks.T.shape, jnp.int32),
            pltpu.SMEM(global_blocks.shape, jnp.int32),
            pltpu.SMEM(win_reach.shape, jnp.int32),
            pltpu.VMEM((tokens, HEAD_DIM), jnp.bfloat16), dma, dma,
        ],
        compiler_params=pltpu.CompilerParams(
            collective_id=0, has_side_effects=True, vmem_limit_bytes=62 * 1024 * 1024
        ),
    )(rand_blocks.T, global_blocks, win_reach, queries[0], out_grad[0], keys[0], values[0])
    pieces = 2
    return pl.pallas_call(
        functools.partial(copy_out, sections, pieces),
        out_shape=shapes,
        in_specs=[vmem, vmem],
        out_specs=(anywhere, anywhere),
        scratch_shapes=[
            pltpu.VMEM((tokens // pieces, queries.shape[2]), jnp.bfloat16),
            dma((2 * pieces,)),
        ],
    )(*(pltpu.with_memory_space_constraint(x, pltpu.VMEM) for x in landing))


def solution(mesh):
    placed = (
        P("section", "seq", "tp"),
        P("section", "seq", None),
        P("section", "seq", None),
        P("section", "seq", "tp"),
        P(),
        P(),
        P(),
    )
    return jax.shard_map(
        on_device,
        mesh=mesh,
        in_specs=placed,
        out_specs=(P("section", "seq", "tp"), P("section", "seq", "tp")),
        check_vma=False,
    )
```

```python
import functools
import math

import jax
import jax.numpy as jnp
from jax import lax
from jax.experimental import pallas as pl
from jax.experimental.pallas import tpu as pltpu
from jax.sharding import PartitionSpec as P

HEAD_DIM = 128
BLOCK_LEN = 64
WINDOW = 1
MESH = pl.DeviceIdType.MESH
NT = (((1,), (1,)), ((), ()))
TN = (((0,), (0,)), ((), ()))


DETOUR = 2
DETOUR_GROUP = 2


def head_cols(h):
    return pl.ds(pl.multiple_of(h * HEAD_DIM, HEAD_DIM), HEAD_DIM)


def kernel(
    sections, shards, groups, repeats, rand_hbm, glob_hbm, reach_hbm,
    q_hbm, do_hbm, k_hbm, v_hbm, outq_ref, outkv_ref,
    q_ref, do_ref, kv_all, stage, sib, part, landed, dq, final,
    g_send, g_recv, f_send, f0_send, f_recv, x_send, x_recv, r_send, r_recv,
    zq_send, zq_recv, zk_send, zk_recv, s_send, s_recv, own_sem, load_sem, table_sem,
    rand_ref, glob_ref, reach_ref, hop, hop_send, hop_recv,
):
    section = lax.axis_index("section")
    me = lax.axis_index("seq")
    t = lax.axis_index("tp")
    peers = shards - 1
    tokens = q_ref.shape[0]
    local_blocks = tokens // BLOCK_LEN
    all_blocks = local_blocks * shards
    scale = HEAD_DIM ** -0.5
    moved = groups - 1
    detours = DETOUR if shards > DETOUR and repeats > DETOUR else 0
    helps = (me > 0) & (me <= detours)
    low = jnp.where(section > 0, 0, moved)
    high = jnp.where(section < sections - 1, groups, moved)

    def rows(shard):
        return pl.ds(pl.multiple_of(shard * tokens, tokens), tokens)

    def remote(src, dst, send, recv, device):
        return pltpu.make_async_remote_copy(
            src_ref=src, dst_ref=dst, send_sem=send, recv_sem=recv,
            device_id=device, device_id_type=MESH,
        )

    def own(half, g, source):
        return pltpu.make_async_copy(
            source.at[:, head_cols(g)], kv_all.at[half, g, rows(me)], own_sem
        )

    def gather(g, d, shard, source=None):
        block = kv_all.at[t, g, rows(shard)]
        source = block if source is None else source.at[:, head_cols(g)]
        to = lax.rem(me + d, shards)
        return remote(source, block, g_send.at[jnp.where(g == low, 0, 1)], g_recv.at[g], {"seq": to})

    def forward(g, d, half):
        block = kv_all.at[half, g, rows(lax.rem(me - d + shards, shards))]
        return remote(block, block, f_send, f_recv.at[g], {"tp": 1 - t})

    def exchange(g):
        return remote(stage.at[1 - t, g], sib.at[g], x_send, x_recv.at[g], {"tp": 1 - t})

    def scatter(g, d):
        to = lax.rem(me + d, shards)
        return remote(
            part.at[g, rows(to)], landed.at[g, d - 1],
            r_send, r_recv.at[g], {"seq": to},
        )

    def hand_query(g, r):
        cols = head_cols(r * groups + g)
        return remote(
            dq.at[:, cols], outq_ref.at[0, :, cols],
            zq_send, zq_recv, {"section": section - 1},
        )

    def detour(r):
        return remote(
            dq.at[:, head_cols(r * groups + DETOUR_GROUP)], hop,
            zq_send, hop_recv, {"seq": r + 1},
        )

    def hand_on():
        cols = head_cols((me - 1) * groups + DETOUR_GROUP)
        return remote(
            hop, outq_ref.at[0, :, cols], hop_send, zq_recv,
            {"section": section - 1, "seq": 0},
        )

    def hand_keyval(g):
        cols = head_cols(g)
        return remote(
            final.at[:, cols], outkv_ref.at[0, :, cols],
            zk_send, zk_recv, {"section": section - 1},
        )

    def hand_input(r, which):
        cols = head_cols(r * groups + moved)
        source, target = ((q_hbm, q_ref), (do_hbm, do_ref))[which]
        return remote(
            source.at[:, cols], target.at[:, cols],
            s_send, s_recv.at[0], {"section": section - 1},
        )

    def hand_shard(source):
        return remote(
            source.at[:, head_cols(moved)], kv_all.at[t, moved, rows(me)],
            s_send, s_recv.at[1], {"section": section - 1},
        )

    def load(r, which):
        cols = pl.ds(r * groups * HEAD_DIM, moved * HEAD_DIM)
        source, target = ((q_hbm, q_ref), (do_hbm, do_ref))[which]
        return pltpu.make_async_copy(source.at[:, cols], target.at[:, cols], load_sem.at[which])

    def arrived(sem, ref):
        remote(ref, ref, sem, sem, {"tp": 1 - t}).wait_recv()

    def left(sem, ref):
        remote(ref, ref, sem, sem, {"tp": 1 - t}).wait_send()

    def loaded(sem, ref):
        pltpu.make_async_copy(ref, ref, sem).wait()

    def pieces(count):
        return kv_all.at[0, pl.ds(0, count), pl.ds(0, peers * tokens)]

    tables = [
        pltpu.make_async_copy(source, target, table_sem.at[i])
        for i, (source, target) in enumerate(
            ((rand_hbm, rand_ref), (glob_hbm, glob_ref), (reach_hbm, reach_ref))
        )
    ]
    barrier = pltpu.get_barrier_semaphore()

    @pl.loop(1, shards)
    def _(d):
        pl.semaphore_signal(
            barrier, inc=1, device_id={"seq": lax.rem(me + d, shards)}, device_id_type=MESH
        )

    pl.semaphore_signal(barrier, inc=1, device_id={"tp": 1 - t}, device_id_type=MESH)

    @pl.when(section < sections - 1)
    def _():
        pl.semaphore_signal(
            barrier, inc=1, device_id={"section": section + 1}, device_id_type=MESH
        )

        @pl.when(me == 0)
        def _():
            for r in range(detours):
                pl.semaphore_signal(
                    barrier, inc=1, device_id={"section": section + 1, "seq": r + 1},
                    device_id_type=MESH,
                )

    for table in tables:
        table.start()

    below = jnp.where(section > 0, 1 + jnp.where(helps, 1, 0), 0)
    pl.semaphore_wait(barrier, peers + 1 + below)

    @pl.when(section > 0)
    def _():
        for half, source in ((0, k_hbm), (1, v_hbm)):

            @pl.when(t == half)
            def _():
                hand_shard(source).start()

    def spread(g):
        for half, source in ((0, k_hbm), (1, v_hbm)):

            @pl.when((g < moved) & (t == half))
            def _():
                @pl.loop(1, shards)
                def _(d):
                    gather(g, d, me, source).start()

        @pl.when(g == moved)
        def _():
            arrived(s_recv.at[1], kv_all.at[t, moved, rows(me)])
            block = kv_all.at[t, g, rows(me)]
            remote(block, block, f0_send, f_recv.at[g], {"tp": 1 - t}).start()

            @pl.loop(1, shards)
            def _(d):
                gather(g, d, me).start()

    def pass_on(g):
        arrived(g_recv.at[g], pieces(1))

        @pl.loop(1, shards)
        def _(d):
            forward(g, d, t).start()

        ahead = jnp.where(g == low, 2, 3)
        begun = jnp.where(g == low, 2, jnp.where(g == low + 1, 2, 3))

        @pl.loop(lax.min(g + begun, high), lax.min(g + ahead + 1, high))
        def _(h):
            spread(h)

    spread(low)

    @pl.when(section > 0)
    def _():
        for r in range(repeats):
            hand_input(r, 0).start()
            hand_input(r, 1).start()

    @pl.when(section > 0)
    def _():
        @pl.loop(0, moved)
        def _(g):
            own(0, g, k_hbm).start()
            own(1, g, v_hbm).start()

        for r in range(repeats):
            load(r, 0).start()
            load(r, 1).start()

    left(g_send.at[0], pieces(1))

    @pl.when(low + 1 < high)
    def _():
        spread(low + 1)

    def send_parts(g):
        arrived(x_recv.at[g], sib.at[g])
        both = stage[t, g].astype(jnp.float32) + sib[g].astype(jnp.float32)
        part[g] = both.astype(jnp.bfloat16)

        @pl.loop(1, shards)
        def _(d):
            scatter(g, d).start()

    for table in tables:
        table.wait()
    chunk = 2
    lag = 3
    width = chunk * tokens
    lane = lax.broadcasted_iota(jnp.int32, (all_blocks, width), 1)
    block_id = lax.broadcasted_iota(jnp.int32, (all_blocks, width), 0)
    lane_block = lax.rem(lane, tokens) // BLOCK_LEN
    lane_head = lane // tokens
    query_block = me * local_blocks + lane_block
    distance = jnp.abs(block_id - query_block)
    always = jnp.zeros((all_blocks, width), jnp.float32)
    for i in range(glob_ref.shape[0]):
        always += (block_id == glob_ref[i]).astype(jnp.float32)
    for i in range(rand_ref.shape[0]):
        for j in range(local_blocks):
            named = (lane_block == j) & (block_id == rand_ref[i, me * local_blocks + j])
            always += named.astype(jnp.float32)

    def finish(g):
        arrived(r_recv.at[g], landed.at[g])
        total = part[g, rows(me), :].astype(jnp.float32)
        for d in range(1, shards):
            total += landed[g, d - 1].astype(jnp.float32)
        total = total.astype(jnp.bfloat16)

        @pl.when(g < moved)
        def _():
            final[:, head_cols(g)] = total
            hand_keyval(g).start()

        @pl.when(g == moved)
        def _():
            outkv_ref[0, :, head_cols(g)] = total

    pass_on(low)

    own_width = repeats * moved * HEAD_DIM

    @pl.when(section > 0)
    def _():
        loaded(load_sem.at[0], q_ref.at[:, pl.ds(0, own_width)])
        loaded(load_sem.at[1], do_ref.at[:, pl.ds(0, own_width)])
        loaded(own_sem, dq.at[:, pl.ds(0, 2 * moved * HEAD_DIM)])

    @pl.loop(low, high)
    def _(g):
        @pl.when(g < moved)
        def _():
            arrived(f_recv.at[g], pieces(1))

        @pl.when(g == moved)
        def _():
            arrived(f_recv.at[g], kv_all.at[0, g])
            arrived(s_recv.at[0], q_ref.at[:, pl.ds(0, 2 * repeats * HEAD_DIM)])

        keys = kv_all[0, g]
        values = kv_all[1, g]
        key_grads = None
        for c in range(repeats // chunk):
            heads = [c * chunk + i for i in range(chunk)]
            query = jnp.concatenate([q_ref[:, head_cols(r * groups + g)] for r in heads], axis=0)
            grad = jnp.concatenate([do_ref[:, head_cols(r * groups + g)] for r in heads], axis=0)
            reach = jnp.zeros((all_blocks, width), jnp.int32)
            for i, r in enumerate(heads):
                reach = jnp.where(lane_head == i, reach_ref[(t * repeats + r) * groups + g], reach)
            window = (distance <= WINDOW) & (distance <= reach)
            count = always + window.astype(jnp.float32)
            bias = jnp.where(
                count > 0, jnp.log(jnp.maximum(count, 1.0)) * (1.0 / math.log(2.0)), -1e30
            )
            scores = lax.dot_general(keys, query, NT, preferred_element_type=jnp.float32)
            scores = scores.reshape(all_blocks, BLOCK_LEN, width) * (scale / math.log(2.0))
            scores = (scores + bias[:, None, :]).reshape(all_blocks * BLOCK_LEN, width)
            row_max = jnp.max(scores, axis=0, keepdims=True)
            terms = jnp.exp2(scores - row_max)
            weights = terms * (1.0 / jnp.sum(terms, axis=0, keepdims=True))
            weight_grads = lax.dot_general(values, grad, NT, preferred_element_type=jnp.float32)
            delta = jnp.sum(weights * weight_grads, axis=0, keepdims=True)
            grads_low = (weights * (weight_grads - delta)).astype(jnp.bfloat16)
            weights_low = weights.astype(jnp.bfloat16)
            query_grads = lax.dot_general(
                grads_low, keys, TN, preferred_element_type=jnp.float32
            )
            query_grads = (query_grads * scale).astype(jnp.bfloat16)

            @pl.when(g < moved)
            def _():
                for i, r in enumerate(heads):
                    dq[:, head_cols(r * groups + g)] = query_grads[i * tokens : (i + 1) * tokens]
                    if r >= detours:
                        hand_query(g, r).start()
                    else:
                        around = (g == DETOUR_GROUP) & (me == 0)

                        @pl.when(around)
                        def _():
                            detour(r).start()

                        @pl.when(jnp.logical_not(around))
                        def _():
                            hand_query(g, r).start()

            @pl.when(g == moved)
            def _():
                for i, r in enumerate(heads):
                    cols = head_cols(r * groups + g)
                    outq_ref[0, :, cols] = query_grads[i * tokens : (i + 1) * tokens]

            if c == 0:

                @pl.when(g + 1 < high)
                def _():
                    pass_on(g + 1)

            dk = jnp.dot(grads_low, query, preferred_element_type=jnp.float32)
            dv = jnp.dot(weights_low, grad, preferred_element_type=jnp.float32)
            key_grads = dk if key_grads is None else key_grads + dk
            value_grads = dv if c == 0 else value_grads + dv
        stage[0, g] = (key_grads * scale).astype(jnp.bfloat16)
        stage[1, g] = value_grads.astype(jnp.bfloat16)
        exchange(g).start()

        @pl.when(g > low)
        def _():
            send_parts(g - 1)

        @pl.when(g >= low + lag)
        def _():
            finish(g - lag)

        @pl.when((g == DETOUR_GROUP + 1) & helps)
        def _():
            arrived(hop_recv, hop)
            hand_on().start()

    send_parts(high - 1)

    @pl.loop(lax.max(low, high - lag), high)
    def _(g):
        finish(g)

    for count, some in (
        (1, section == 0),
        (groups - 1, section == sections - 1),
        (groups, (section > 0) & (section < sections - 1)),
    ):

        @pl.when(some)
        def _():
            if count > 1:
                left(g_send.at[1], pieces(count - 1))
            left(f_send, pieces(count))
            left(r_send, pieces(count))
            left(x_send, sib.at[pl.ds(0, count)])

    @pl.when(section > 0)
    def _():
        left(s_send, q_ref.at[:, pl.ds(0, (2 * repeats + 1) * HEAD_DIM)])
        left(zq_send, dq.at[:, pl.ds(0, own_width)])

        @pl.when(helps)
        def _():
            left(hop_send, hop)

        left(zk_send, final.at[:, pl.ds(0, moved * HEAD_DIM)])

    @pl.when(section < sections - 1)
    def _():
        left(f0_send, kv_all.at[t, moved, rows(me)])
        arrived(zq_recv, outq_ref.at[0, :, pl.ds(0, own_width)])
        arrived(zk_recv, outkv_ref.at[0, :, pl.ds(0, moved * HEAD_DIM)])


def copy_out(sections, pieces, q_in, kv_in, q_out, kv_out, blank, out_sem):
    section = lax.axis_index("section")
    size = q_in.shape[1] // pieces
    width = kv_in.shape[2]

    def stores(held):
        copies = []
        for k, (source, target) in enumerate(((q_in, q_out), (kv_in, kv_out))):
            for i in range(pieces):
                piece = pl.ds(i * size, size)
                src = source.at[0, piece] if held is None else held.at[:, pl.ds(0, source.shape[2])]
                copies.append(
                    pltpu.make_async_copy(src, target.at[0, piece], out_sem.at[k * pieces + i])
                )
        return copies

    @pl.when(section < sections - 1)
    def _():
        for store in stores(None):
            store.start()

    @pl.when(section == sections - 1)
    def _():
        blank[...] = jnp.zeros_like(blank)
        for store in stores(blank):
            store.start()

    for store in stores(None):
        store.wait()


def on_device(queries, keys, values, out_grad, rand_blocks, global_blocks, win_reach):
    sections = lax.axis_size("section")
    shards = lax.axis_size("seq")
    tokens = queries.shape[1]
    kv_width = keys.shape[2]
    groups = kv_width // HEAD_DIM
    repeats = queries.shape[2] // kv_width
    length = tokens * shards
    peers = shards - 1
    dma = pltpu.SemaphoreType.DMA
    vmem = pl.BlockSpec(memory_space=pltpu.VMEM)
    smem = pl.BlockSpec(memory_space=pltpu.SMEM)
    anywhere = pl.BlockSpec(memory_space=pltpu.HBM)
    shapes = (
        jax.ShapeDtypeStruct(queries.shape, jnp.bfloat16),
        jax.ShapeDtypeStruct((1, tokens, kv_width), jnp.bfloat16),
    )
    landing = pl.pallas_call(
        functools.partial(kernel, sections, shards, groups, repeats),
        out_shape=tuple(pltpu.VMEM(x.shape, x.dtype) for x in shapes),
        in_specs=[anywhere] * 7,
        out_specs=(vmem, vmem),
        scratch_shapes=[
            pltpu.VMEM((tokens, queries.shape[2]), jnp.bfloat16),
            pltpu.VMEM((tokens, queries.shape[2]), jnp.bfloat16),
            pltpu.VMEM((2, groups, length, HEAD_DIM), jnp.bfloat16),
            pltpu.VMEM((2, groups, length, HEAD_DIM), jnp.bfloat16),
            pltpu.VMEM((groups, length, HEAD_DIM), jnp.bfloat16),
            pltpu.VMEM((groups, length, HEAD_DIM), jnp.bfloat16),
            pltpu.VMEM((groups, peers, tokens, HEAD_DIM), jnp.bfloat16),
            pltpu.VMEM((tokens, queries.shape[2]), jnp.bfloat16),
            pltpu.VMEM((tokens, kv_width), jnp.bfloat16),
            dma((2,)), dma((groups,)),
            dma, dma, dma((groups,)),
            dma, dma((groups,)),
            dma, dma((groups,)),
            dma, dma, dma, dma,
            dma, dma((2,)),
            dma, dma((2,)), dma((3,)),
            pltpu.SMEM(rand_blocks.T.shape, jnp.int32),
            pltpu.SMEM(global_blocks.shape, jnp.int32),
            pltpu.SMEM(win_reach.shape, jnp.int32),
            pltpu.VMEM((tokens, HEAD_DIM), jnp.bfloat16), dma, dma,
        ],
        compiler_params=pltpu.CompilerParams(
            collective_id=0, has_side_effects=True, vmem_limit_bytes=62 * 1024 * 1024
        ),
    )(rand_blocks.T, global_blocks, win_reach, queries[0], out_grad[0], keys[0], values[0])
    pieces = 2
    return pl.pallas_call(
        functools.partial(copy_out, sections, pieces),
        out_shape=shapes,
        in_specs=[vmem, vmem],
        out_specs=(anywhere, anywhere),
        scratch_shapes=[
            pltpu.VMEM((tokens // pieces, queries.shape[2]), jnp.bfloat16),
            dma((2 * pieces,)),
        ],
    )(*(pltpu.with_memory_space_constraint(x, pltpu.VMEM) for x in landing))


def solution(mesh):
    placed = (
        P("section", "seq", "tp"),
        P("section", "seq", None),
        P("section", "seq", None),
        P("section", "seq", "tp"),
        P(),
        P(),
        P(),
    )
    return jax.shard_map(
        on_device,
        mesh=mesh,
        in_specs=placed,
        out_specs=(P("section", "seq", "tp"), P("section", "seq", "tp")),
        check_vma=False,
    )
```

```python
import functools
import math

import jax
import jax.numpy as jnp
from jax import lax
from jax.experimental import pallas as pl
from jax.experimental.pallas import tpu as pltpu
from jax.sharding import PartitionSpec as P

HEAD_DIM = 128
BLOCK_LEN = 64
WINDOW = 1
MESH = pl.DeviceIdType.MESH
NT = (((1,), (1,)), ((), ()))
TN = (((0,), (0,)), ((), ()))


DETOUR = 2
DETOUR_GROUP = 2


def head_cols(h):
    return pl.ds(pl.multiple_of(h * HEAD_DIM, HEAD_DIM), HEAD_DIM)


def kernel(
    sections, shards, groups, repeats, rand_hbm, glob_hbm, reach_hbm,
    q_hbm, do_hbm, k_hbm, v_hbm, outq_ref, outkv_ref,
    q_ref, do_ref, kv_all, stage, sib, part, landed, dq, final,
    g_send, g_recv, f_send, f0_send, f_recv, x_send, x_recv, r_send, r_recv,
    zq_send, zq_recv, zk_send, zk_recv, s_send, s_recv, own_sem, load_sem, table_sem,
    rand_ref, glob_ref, reach_ref, hop, hop_send, hop_recv,
):
    section = lax.axis_index("section")
    me = lax.axis_index("seq")
    t = lax.axis_index("tp")
    peers = shards - 1
    tokens = q_ref.shape[0]
    local_blocks = tokens // BLOCK_LEN
    all_blocks = local_blocks * shards
    scale = HEAD_DIM ** -0.5
    moved = groups - 1
    detours = DETOUR if shards > DETOUR and repeats > DETOUR else 0
    helps = (me > 0) & (me <= detours)
    low = jnp.where(section > 0, 0, moved)
    high = jnp.where(section < sections - 1, groups, moved)

    def rows(shard):
        return pl.ds(pl.multiple_of(shard * tokens, tokens), tokens)

    def remote(src, dst, send, recv, device):
        return pltpu.make_async_remote_copy(
            src_ref=src, dst_ref=dst, send_sem=send, recv_sem=recv,
            device_id=device, device_id_type=MESH,
        )

    def own(half, g, source):
        return pltpu.make_async_copy(
            source.at[:, head_cols(g)], kv_all.at[half, g, rows(me)], own_sem
        )

    def gather(g, d, shard, source=None):
        block = kv_all.at[t, g, rows(shard)]
        source = block if source is None else source.at[:, head_cols(g)]
        to = lax.rem(me + d, shards)
        return remote(source, block, g_send.at[jnp.where(g == low, 0, 1)], g_recv.at[g], {"seq": to})

    def forward(g, d, half):
        block = kv_all.at[half, g, rows(lax.rem(me - d + shards, shards))]
        return remote(block, block, f_send, f_recv.at[g], {"tp": 1 - t})

    def exchange(g):
        return remote(stage.at[1 - t, g], sib.at[g], x_send, x_recv.at[g], {"tp": 1 - t})

    def scatter(g, d):
        to = lax.rem(me + d, shards)
        return remote(
            part.at[g, rows(to)], landed.at[g, d - 1],
            r_send, r_recv.at[g], {"seq": to},
        )

    def hand_query(g, r):
        cols = head_cols(r * groups + g)
        return remote(
            dq.at[:, cols], outq_ref.at[0, :, cols],
            zq_send, zq_recv, {"section": section - 1},
        )

    def detour(r):
        return remote(
            dq.at[:, head_cols(r * groups + DETOUR_GROUP - 1 + r)], hop,
            zq_send, hop_recv, {"seq": r + 1},
        )

    def hand_on():
        cols = head_cols((me - 1) * groups + DETOUR_GROUP - 1 + (me - 1))
        return remote(
            hop, outq_ref.at[0, :, cols], hop_send, zq_recv,
            {"section": section - 1, "seq": 0},
        )

    def hand_keyval(g):
        cols = head_cols(g)
        return remote(
            final.at[:, cols], outkv_ref.at[0, :, cols],
            zk_send, zk_recv, {"section": section - 1},
        )

    def hand_input(r, which):
        cols = head_cols(r * groups + moved)
        source, target = ((q_hbm, q_ref), (do_hbm, do_ref))[which]
        return remote(
            source.at[:, cols], target.at[:, cols],
            s_send, s_recv.at[0], {"section": section - 1},
        )

    def hand_shard(source):
        return remote(
            source.at[:, head_cols(moved)], kv_all.at[t, moved, rows(me)],
            s_send, s_recv.at[1], {"section": section - 1},
        )

    def load(r, which):
        cols = pl.ds(r * groups * HEAD_DIM, moved * HEAD_DIM)
        source, target = ((q_hbm, q_ref), (do_hbm, do_ref))[which]
        return pltpu.make_async_copy(source.at[:, cols], target.at[:, cols], load_sem.at[which])

    def arrived(sem, ref):
        remote(ref, ref, sem, sem, {"tp": 1 - t}).wait_recv()

    def left(sem, ref):
        remote(ref, ref, sem, sem, {"tp": 1 - t}).wait_send()

    def loaded(sem, ref):
        pltpu.make_async_copy(ref, ref, sem).wait()

    def pieces(count):
        return kv_all.at[0, pl.ds(0, count), pl.ds(0, peers * tokens)]

    tables = [
        pltpu.make_async_copy(source, target, table_sem.at[i])
        for i, (source, target) in enumerate(
            ((rand_hbm, rand_ref), (glob_hbm, glob_ref), (reach_hbm, reach_ref))
        )
    ]
    barrier = pltpu.get_barrier_semaphore()

    @pl.loop(1, shards)
    def _(d):
        pl.semaphore_signal(
            barrier, inc=1, device_id={"seq": lax.rem(me + d, shards)}, device_id_type=MESH
        )

    pl.semaphore_signal(barrier, inc=1, device_id={"tp": 1 - t}, device_id_type=MESH)

    @pl.when(section < sections - 1)
    def _():
        pl.semaphore_signal(
            barrier, inc=1, device_id={"section": section + 1}, device_id_type=MESH
        )

        @pl.when(me == 0)
        def _():
            for r in range(detours):
                pl.semaphore_signal(
                    barrier, inc=1, device_id={"section": section + 1, "seq": r + 1},
                    device_id_type=MESH,
                )

    for table in tables:
        table.start()

    below = jnp.where(section > 0, 1 + jnp.where(helps, 1, 0), 0)
    pl.semaphore_wait(barrier, peers + 1 + below)

    @pl.when(section > 0)
    def _():
        for half, source in ((0, k_hbm), (1, v_hbm)):

            @pl.when(t == half)
            def _():
                hand_shard(source).start()

    def spread(g):
        for half, source in ((0, k_hbm), (1, v_hbm)):

            @pl.when((g < moved) & (t == half))
            def _():
                @pl.loop(1, shards)
                def _(d):
                    gather(g, d, me, source).start()

        @pl.when(g == moved)
        def _():
            arrived(s_recv.at[1], kv_all.at[t, moved, rows(me)])
            block = kv_all.at[t, g, rows(me)]
            remote(block, block, f0_send, f_recv.at[g], {"tp": 1 - t}).start()

            @pl.loop(1, shards)
            def _(d):
                gather(g, d, me).start()

    def pass_on(g):
        arrived(g_recv.at[g], pieces(1))

        @pl.loop(1, shards)
        def _(d):
            forward(g, d, t).start()

        ahead = jnp.where(g == low, 2, 3)
        begun = jnp.where(g == low, 2, jnp.where(g == low + 1, 2, 3))

        @pl.loop(lax.min(g + begun, high), lax.min(g + ahead + 1, high))
        def _(h):
            spread(h)

    spread(low)

    @pl.when(section > 0)
    def _():
        for r in range(repeats):
            hand_input(r, 0).start()
            hand_input(r, 1).start()

    @pl.when(section > 0)
    def _():
        @pl.loop(0, moved)
        def _(g):
            own(0, g, k_hbm).start()
            own(1, g, v_hbm).start()

        for r in range(repeats):
            load(r, 0).start()
            load(r, 1).start()

    left(g_send.at[0], pieces(1))

    @pl.when(low + 1 < high)
    def _():
        spread(low + 1)

    def send_parts(g):
        arrived(x_recv.at[g], sib.at[g])
        both = stage[t, g].astype(jnp.float32) + sib[g].astype(jnp.float32)
        part[g] = both.astype(jnp.bfloat16)

        @pl.loop(1, shards)
        def _(d):
            scatter(g, d).start()

    for table in tables:
        table.wait()
    chunk = 2
    lag = 3
    width = chunk * tokens
    lane = lax.broadcasted_iota(jnp.int32, (all_blocks, width), 1)
    block_id = lax.broadcasted_iota(jnp.int32, (all_blocks, width), 0)
    lane_block = lax.rem(lane, tokens) // BLOCK_LEN
    lane_head = lane // tokens
    query_block = me * local_blocks + lane_block
    distance = jnp.abs(block_id - query_block)
    always = jnp.zeros((all_blocks, width), jnp.float32)
    for i in range(glob_ref.shape[0]):
        always += (block_id == glob_ref[i]).astype(jnp.float32)
    for i in range(rand_ref.shape[0]):
        for j in range(local_blocks):
            named = (lane_block == j) & (block_id == rand_ref[i, me * local_blocks + j])
            always += named.astype(jnp.float32)

    def finish(g):
        arrived(r_recv.at[g], landed.at[g])
        total = part[g, rows(me), :].astype(jnp.float32)
        for d in range(1, shards):
            total += landed[g, d - 1].astype(jnp.float32)
        total = total.astype(jnp.bfloat16)

        @pl.when(g < moved)
        def _():
            final[:, head_cols(g)] = total
            hand_keyval(g).start()

        @pl.when(g == moved)
        def _():
            outkv_ref[0, :, head_cols(g)] = total

    pass_on(low)

    own_width = repeats * moved * HEAD_DIM

    @pl.when(section > 0)
    def _():
        loaded(load_sem.at[0], q_ref.at[:, pl.ds(0, own_width)])
        loaded(load_sem.at[1], do_ref.at[:, pl.ds(0, own_width)])
        loaded(own_sem, dq.at[:, pl.ds(0, 2 * moved * HEAD_DIM)])

    @pl.loop(low, high)
    def _(g):
        @pl.when(g < moved)
        def _():
            arrived(f_recv.at[g], pieces(1))

        @pl.when(g == moved)
        def _():
            arrived(f_recv.at[g], kv_all.at[0, g])
            arrived(s_recv.at[0], q_ref.at[:, pl.ds(0, 2 * repeats * HEAD_DIM)])

        keys = kv_all[0, g]
        values = kv_all[1, g]
        key_grads = None
        for c in range(repeats // chunk):
            heads = [c * chunk + i for i in range(chunk)]
            query = jnp.concatenate([q_ref[:, head_cols(r * groups + g)] for r in heads], axis=0)
            grad = jnp.concatenate([do_ref[:, head_cols(r * groups + g)] for r in heads], axis=0)
            reach = jnp.zeros((all_blocks, width), jnp.int32)
            for i, r in enumerate(heads):
                reach = jnp.where(lane_head == i, reach_ref[(t * repeats + r) * groups + g], reach)
            window = (distance <= WINDOW) & (distance <= reach)
            count = always + window.astype(jnp.float32)
            bias = jnp.where(
                count > 0, jnp.log(jnp.maximum(count, 1.0)) * (1.0 / math.log(2.0)), -1e30
            )
            scores = lax.dot_general(keys, query, NT, preferred_element_type=jnp.float32)
            scores = scores.reshape(all_blocks, BLOCK_LEN, width) * (scale / math.log(2.0))
            scores = (scores + bias[:, None, :]).reshape(all_blocks * BLOCK_LEN, width)
            row_max = jnp.max(scores, axis=0, keepdims=True)
            terms = jnp.exp2(scores - row_max)
            weights = terms * (1.0 / jnp.sum(terms, axis=0, keepdims=True))
            weight_grads = lax.dot_general(values, grad, NT, preferred_element_type=jnp.float32)
            delta = jnp.sum(weights * weight_grads, axis=0, keepdims=True)
            grads_low = (weights * (weight_grads - delta)).astype(jnp.bfloat16)
            weights_low = weights.astype(jnp.bfloat16)
            query_grads = lax.dot_general(
                grads_low, keys, TN, preferred_element_type=jnp.float32
            )
            query_grads = (query_grads * scale).astype(jnp.bfloat16)

            @pl.when(g < moved)
            def _():
                for i, r in enumerate(heads):
                    dq[:, head_cols(r * groups + g)] = query_grads[i * tokens : (i + 1) * tokens]
                    if r >= detours:
                        hand_query(g, r).start()
                    else:
                        around = (g == DETOUR_GROUP - 1 + r) & (me == 0)

                        @pl.when(around)
                        def _():
                            detour(r).start()

                        @pl.when(jnp.logical_not(around))
                        def _():
                            hand_query(g, r).start()

            @pl.when(g == moved)
            def _():
                for i, r in enumerate(heads):
                    cols = head_cols(r * groups + g)
                    outq_ref[0, :, cols] = query_grads[i * tokens : (i + 1) * tokens]

            if c == 0:

                @pl.when(g + 1 < high)
                def _():
                    pass_on(g + 1)

            dk = jnp.dot(grads_low, query, preferred_element_type=jnp.float32)
            dv = jnp.dot(weights_low, grad, preferred_element_type=jnp.float32)
            key_grads = dk if key_grads is None else key_grads + dk
            value_grads = dv if c == 0 else value_grads + dv
        stage[0, g] = (key_grads * scale).astype(jnp.bfloat16)
        stage[1, g] = value_grads.astype(jnp.bfloat16)
        exchange(g).start()

        @pl.when(g > low)
        def _():
            send_parts(g - 1)

        @pl.when(g >= low + lag)
        def _():
            finish(g - lag)

        @pl.when((g == DETOUR_GROUP - 1 + (me - 1) + 1) & helps)
        def _():
            arrived(hop_recv, hop)
            hand_on().start()

    send_parts(high - 1)

    @pl.loop(lax.max(low, high - lag), high)
    def _(g):
        finish(g)

    for count, some in (
        (1, section == 0),
        (groups - 1, section == sections - 1),
        (groups, (section > 0) & (section < sections - 1)),
    ):

        @pl.when(some)
        def _():
            if count > 1:
                left(g_send.at[1], pieces(count - 1))
            left(f_send, pieces(count))
            left(r_send, pieces(count))
            left(x_send, sib.at[pl.ds(0, count)])

    @pl.when(section > 0)
    def _():
        left(s_send, q_ref.at[:, pl.ds(0, (2 * repeats + 1) * HEAD_DIM)])
        left(zq_send, dq.at[:, pl.ds(0, own_width)])

        @pl.when(helps)
        def _():
            left(hop_send, hop)

        left(zk_send, final.at[:, pl.ds(0, moved * HEAD_DIM)])

    @pl.when(section < sections - 1)
    def _():
        left(f0_send, kv_all.at[t, moved, rows(me)])
        arrived(zq_recv, outq_ref.at[0, :, pl.ds(0, own_width)])
        arrived(zk_recv, outkv_ref.at[0, :, pl.ds(0, moved * HEAD_DIM)])


def copy_out(sections, pieces, q_in, kv_in, q_out, kv_out, blank, out_sem):
    section = lax.axis_index("section")
    size = q_in.shape[1] // pieces
    width = kv_in.shape[2]

    def stores(held):
        copies = []
        for k, (source, target) in enumerate(((q_in, q_out), (kv_in, kv_out))):
            for i in range(pieces):
                piece = pl.ds(i * size, size)
                src = source.at[0, piece] if held is None else held.at[:, pl.ds(0, source.shape[2])]
                copies.append(
                    pltpu.make_async_copy(src, target.at[0, piece], out_sem.at[k * pieces + i])
                )
        return copies

    @pl.when(section < sections - 1)
    def _():
        for store in stores(None):
            store.start()

    @pl.when(section == sections - 1)
    def _():
        blank[...] = jnp.zeros_like(blank)
        for store in stores(blank):
            store.start()

    for store in stores(None):
        store.wait()


def on_device(queries, keys, values, out_grad, rand_blocks, global_blocks, win_reach):
    sections = lax.axis_size("section")
    shards = lax.axis_size("seq")
    tokens = queries.shape[1]
    kv_width = keys.shape[2]
    groups = kv_width // HEAD_DIM
    repeats = queries.shape[2] // kv_width
    length = tokens * shards
    peers = shards - 1
    dma = pltpu.SemaphoreType.DMA
    vmem = pl.BlockSpec(memory_space=pltpu.VMEM)
    smem = pl.BlockSpec(memory_space=pltpu.SMEM)
    anywhere = pl.BlockSpec(memory_space=pltpu.HBM)
    shapes = (
        jax.ShapeDtypeStruct(queries.shape, jnp.bfloat16),
        jax.ShapeDtypeStruct((1, tokens, kv_width), jnp.bfloat16),
    )
    landing = pl.pallas_call(
        functools.partial(kernel, sections, shards, groups, repeats),
        out_shape=tuple(pltpu.VMEM(x.shape, x.dtype) for x in shapes),
        in_specs=[anywhere] * 7,
        out_specs=(vmem, vmem),
        scratch_shapes=[
            pltpu.VMEM((tokens, queries.shape[2]), jnp.bfloat16),
            pltpu.VMEM((tokens, queries.shape[2]), jnp.bfloat16),
            pltpu.VMEM((2, groups, length, HEAD_DIM), jnp.bfloat16),
            pltpu.VMEM((2, groups, length, HEAD_DIM), jnp.bfloat16),
            pltpu.VMEM((groups, length, HEAD_DIM), jnp.bfloat16),
            pltpu.VMEM((groups, length, HEAD_DIM), jnp.bfloat16),
            pltpu.VMEM((groups, peers, tokens, HEAD_DIM), jnp.bfloat16),
            pltpu.VMEM((tokens, queries.shape[2]), jnp.bfloat16),
            pltpu.VMEM((tokens, kv_width), jnp.bfloat16),
            dma((2,)), dma((groups,)),
            dma, dma, dma((groups,)),
            dma, dma((groups,)),
            dma, dma((groups,)),
            dma, dma, dma, dma,
            dma, dma((2,)),
            dma, dma((2,)), dma((3,)),
            pltpu.SMEM(rand_blocks.T.shape, jnp.int32),
            pltpu.SMEM(global_blocks.shape, jnp.int32),
            pltpu.SMEM(win_reach.shape, jnp.int32),
            pltpu.VMEM((tokens, HEAD_DIM), jnp.bfloat16), dma, dma,
        ],
        compiler_params=pltpu.CompilerParams(
            collective_id=0, has_side_effects=True, vmem_limit_bytes=62 * 1024 * 1024
        ),
    )(rand_blocks.T, global_blocks, win_reach, queries[0], out_grad[0], keys[0], values[0])
    pieces = 2
    return pl.pallas_call(
        functools.partial(copy_out, sections, pieces),
        out_shape=shapes,
        in_specs=[vmem, vmem],
        out_specs=(anywhere, anywhere),
        scratch_shapes=[
            pltpu.VMEM((tokens // pieces, queries.shape[2]), jnp.bfloat16),
            dma((2 * pieces,)),
        ],
    )(*(pltpu.with_memory_space_constraint(x, pltpu.VMEM) for x in landing))


def solution(mesh):
    placed = (
        P("section", "seq", "tp"),
        P("section", "seq", None),
        P("section", "seq", None),
        P("section", "seq", "tp"),
        P(),
        P(),
        P(),
    )
    return jax.shard_map(
        on_device,
        mesh=mesh,
        in_specs=placed,
        out_specs=(P("section", "seq", "tp"), P("section", "seq", "tp")),
        check_vma=False,
    )
```
